512 devices in a mesh: dp: 32 (over z, core), seq: 16 (over y, x).
Axes of the slice: x: 4, y: 4, z: 16, core: 2. Of those that a mesh axis runs over, the one named last changes fastest.
Arguments:
- tokens: bfloat16 [65536, 1280], P(('dp', 'seq')), parts along dimension 0, may hold values from -6 to 6
- segment_ids: int32 [65536], P('dp'), parts along dimension 0, may hold values from 0 to 31, as said below
- w_qkv: bfloat16 [1280, 3840], P(None, 'seq')
- w_out: bfloat16 [1280, 1280], P('seq'), may hold values from -0.15625 to 0.15625
- w_merge: bfloat16 [5120, 4096], P(None, 'seq'), may hold values from -0.078125 to 0.078125
- gain_attn: float32 [1280], replicated, may hold values from 0.1 to 1.9
- gain_merge: float32 [1280], replicated, may hold values from 0.1 to 1.9
Outputs:
- merged_out: bfloat16 [16384, 4096], P(('dp', 'seq')), parts along dimension 0
The draws below stay inside these ranges and needn't reach their ends.
There are 32 independent parts, one for each index of `dp`. The reference program is written for one: setup_inputs(seed, part) draws one part's arguments, and reference() takes and returns one part's arrays. A program takes and returns all parts, laid end to end along the dimension named above; an argument that names none is the same for every part. Nothing has to cross between parts.
Inputs may be any that keep to these rules, and one draw needn't show every extreme that they name: `segment_ids`: Non-decreasing along the packed tokens, starting at 0, rising by 0 or 1 from one token to the next, and equal within every aligned group of 4 tokens (an image's 2x2 patch blocks are stored together). There are exactly 32 images.
All inputs are finite; a program needn't handle non-finite values.
Results may differ from the reference program's by a relative error of at most 0.011.
Values may be sent and summed in bfloat16 or wider, within the bound.
No kernel may reach another device: no remote copies, remote signals or barrier semaphores. Data moves between devices by JAX's collectives and lax.ppermute only.
A program may use at most 64 MiB of HBM per device.

```python
import jax
import jax.numpy as jnp
from jax import lax

D = 1280
HEADS = 16
HEAD_DIM = 80
OUT = 4096
TOK_DEV = 128
TOKENS = 2048
MERGED = 512


def packed_layout(key):
    block_count = TOKENS // 4
    image_count = 2 * (TOKENS // TOK_DEV)
    window = block_count // 2
    window_start = jax.random.randint(jax.random.fold_in(key, 1), (), 0, block_count - window + 1).astype(jnp.int32)
    position = jnp.arange(block_count, dtype=jnp.int32)
    ranks = jax.random.permutation(jax.random.fold_in(key, 2), block_count).astype(jnp.int32)
    barred = (position == 0) | (position > window_start) & (position < window_start + window)
    scored = ranks + barred.astype(jnp.int32) * block_count
    chosen = jnp.argsort(scored)[:image_count - 1]
    starts = jnp.zeros((block_count,), jnp.int32).at[chosen].set(1)
    image_ids = jnp.cumsum(starts).astype(jnp.int32)
    return (jnp.repeat(image_ids, 4).astype(jnp.int32), window_start, window)


def draw_segment_ids(key, part):
    layout = packed_layout(jax.random.fold_in(key, 11))
    return layout[0]


def draw_tokens(key, part):
    layout = packed_layout(jax.random.fold_in(key, 11))
    window_start = layout[1]
    window = layout[2]
    half_window = window // 2
    block_of = jnp.arange(TOKENS, dtype=jnp.int32) // 4
    first_half = (block_of >= window_start) & (block_of < window_start + half_window)
    second_half = (block_of >= window_start + half_window) & (block_of < window_start + window)
    sign_field = first_half.astype(jnp.float32) - second_half.astype(jnp.float32)
    direction = jax.random.uniform(jax.random.fold_in(key, 12), (D,), jnp.float32, -1.0, 1.0)
    base = jnp.clip(jax.random.normal(jax.random.fold_in(key, 13), (TOKENS, D), jnp.float32), -4.0, 4.0)
    shifted = base + 2.0 * sign_field[:, None] * direction[None, :]
    return shifted.astype(jnp.bfloat16)


def draw_w_qkv(key, part):
    base = jax.random.normal(key, (D, HEADS, 3, HEAD_DIM), jnp.float32) * D ** (-0.5)
    return base.reshape(D, 3 * D).astype(jnp.bfloat16)


def block_scale(key, extent, cuts, low, largest):
    def one(axis_at, parts):
        heights = jax.random.uniform(jax.random.fold_in(jax.random.fold_in(key, 6), axis_at), (parts,), jnp.float32, low / len(cuts), largest / len(cuts))
        return jnp.repeat(jnp.exp(heights), extent[axis_at] // parts).reshape((-1,) + (1,) * (len(extent) - axis_at - 1))

    level = one(*cuts[0])
    for cut in cuts[1:]:
        level = level * one(*cut)
    return level


def scatter_about(key, dims, spread, limit, pieces=(), kind=jnp.bfloat16):
    gain = block_scale(key, dims, pieces, -0.22, 0.18) if pieces else 1.0
    array = jax.random.normal(key, dims, jnp.float32) * spread * gain
    return jnp.minimum(jnp.maximum(array, -limit), limit).astype(kind)


def setup_inputs(seed: int = 0, part: int = 0) -> dict:
    arg_keys = jax.random.split(jax.random.key(seed), 8)
    own_keys = jax.random.split(jax.random.fold_in(arg_keys[7], part), 8)
    return {
        "tokens": draw_tokens(jax.random.fold_in(jax.random.fold_in(arg_keys[7], part), 71), part),
        "segment_ids": draw_segment_ids(jax.random.fold_in(jax.random.fold_in(arg_keys[7], part), 71), part),
        "w_qkv": draw_w_qkv(jax.random.fold_in(arg_keys[7], 71), part),
        "w_out": scatter_about(arg_keys[3], (D, D), D ** -0.5, 0.15625, ((0, 16),)),
        "w_merge": scatter_about(arg_keys[4], (4 * D, OUT), (4 * D) ** -0.5, 0.078125, ((1, 16),)),
        "gain_attn": jnp.clip(1.0 + 0.18 * jax.random.normal(arg_keys[5], (D,), jnp.float32), 0.1, 1.9),
        "gain_merge": jnp.clip(1.0 + 0.18 * jax.random.normal(arg_keys[6], (D,), jnp.float32), 0.1, 1.9),
    }


def layer_norm(vector, scale_gain):
    average = lax.optimization_barrier(jnp.mean(vector, axis=-1, keepdims=True))
    centred = vector - average
    spread_sq = lax.optimization_barrier(jnp.mean(centred * centred, axis=-1, keepdims=True))
    return centred * lax.rsqrt(spread_sq + 1e-06) * scale_gain.astype(jnp.float32)

def reference(tokens, segment_ids, w_qkv, w_out, w_merge, gain_attn, gain_merge):
    residual = tokens.astype(jnp.float32)
    normed = layer_norm(residual, gain_attn).astype(jnp.bfloat16)
    qkv = jnp.dot(normed, w_qkv, preferred_element_type=jnp.float32).astype(jnp.bfloat16)
    per_head = jnp.moveaxis(qkv.reshape(TOKENS, HEADS, 3, HEAD_DIM), 1, 0)
    same_image = segment_ids[:, None] == segment_ids[None, :]

    def one_head(head_block):
        queries = head_block[:, 0, :]
        key_rows = head_block[:, 1, :]
        value_rows = head_block[:, 2, :]
        scores = jnp.dot(queries, key_rows.T, preferred_element_type=jnp.float32) * HEAD_DIM ** (-0.5)
        scores = jnp.where(same_image, scores, -jnp.inf)
        row_max = lax.optimization_barrier(jnp.max(scores, axis=-1, keepdims=True))
        expo = jnp.where(same_image, jnp.exp(scores - row_max), 0.0)
        row_sum = lax.optimization_barrier(jnp.sum(expo, axis=-1, keepdims=True))
        probs = expo.astype(jnp.bfloat16)
        result = jnp.dot(probs, value_rows, preferred_element_type=jnp.float32) / row_sum
        return result.astype(jnp.bfloat16)
    heads_out = lax.map(one_head, per_head)
    attended = jnp.moveaxis(heads_out, 0, 1).reshape(TOKENS, D)
    hidden = residual + jnp.dot(attended, w_out, preferred_element_type=jnp.float32)
    normed_two = layer_norm(hidden, gain_merge).astype(jnp.bfloat16)
    merged = normed_two.reshape(MERGED, 4 * D)
    return jnp.dot(merged, w_merge, preferred_element_type=jnp.float32).astype(jnp.bfloat16)
```

```python
import functools

import jax
import jax.numpy as jnp
from jax import lax
from jax.experimental import pallas as pl
from jax.experimental.pallas import tpu as pltpu
from jax.sharding import Mesh
from jax.sharding import PartitionSpec as P

D = 1280
HEADS = 16
HEAD_DIM = 80
TQ = 256
TK = 256
LOG2E = 1.4426950408889634


def layer_norm(vector, scale_gain):
    average = jnp.mean(vector, axis=-1, keepdims=True)
    centred = vector - average
    spread_sq = jnp.mean(centred * centred, axis=-1, keepdims=True)
    return centred * lax.rsqrt(spread_sq + 1e-06) * scale_gain


def broadcast_a2a(block, axes, count):
    spread = jnp.broadcast_to(block[None], (count,) + block.shape)
    return lax.all_to_all(spread, axes, split_axis=0, concat_axis=0, tiled=True)


def swap_cores(value):
    return lax.ppermute(value, "c", [(0, 1), (1, 0)])


def shift_rows(value, step, rows):
    return lax.ppermute(value, "y", [(at, (at + step) % rows) for at in range(rows)])


def attention_kernel(bounds, qkv, seg_col, seg_row, out, keys, seg_wide):
    tiles, _, chunk = qkv.shape
    step = pl.program_id(0)
    per_chunk = chunk // TK

    @pl.when(step == 0)
    def _():
        for index in range(tiles):
            keys[index * chunk:(index + 1) * chunk, :] = qkv[index, HEAD_DIM:2 * HEAD_DIM, :].T
        seg_wide[...] = jnp.broadcast_to(seg_col[...], seg_wide.shape)

    part = step // (chunk // TQ)
    offset = pl.multiple_of((step % (chunk // TQ)) * TQ, TQ)
    queries = qkv[part, 0:HEAD_DIM, pl.ds(offset, TQ)]
    query_seg = seg_row[0:1, pl.ds(pl.multiple_of(step * TQ, TQ), TQ)]
    factor = (HEAD_DIM ** -0.5) * LOG2E

    def body(tile, carry):
        top, total, acc = carry
        start = pl.multiple_of(tile * TK, TK)
        scores = lax.dot_general(
            keys[pl.ds(start, TK), :], queries, (((1,), (0,)), ((), ())),
            preferred_element_type=jnp.float32)
        wide = seg_wide[pl.ds(start, TK), :]
        same = jnp.concatenate([wide] * (TQ // 128), axis=1) == query_seg
        scores = jnp.where(same, scores, -jnp.inf)
        new_top = jnp.maximum(top, jnp.max(scores, axis=0, keepdims=True))
        safe = jnp.where(new_top == -jnp.inf, 0.0, new_top)
        decay = jnp.exp2((top - safe) * factor)
        expo = jnp.exp2((scores - safe) * factor)
        total = total * decay + jnp.sum(expo, axis=0, keepdims=True)
        values = qkv[tile // per_chunk, 2 * HEAD_DIM:3 * HEAD_DIM,
                     pl.ds(pl.multiple_of((tile % per_chunk) * TK, TK), TK)]
        acc = acc * decay + lax.dot_general(
            values, expo.astype(jnp.bfloat16), (((1,), (0,)), ((), ())),
            preferred_element_type=jnp.float32)
        return new_top, total, acc

    first, last = bounds[0, step], bounds[1, step]
    top, total, acc = lax.fori_loop(
        first, last, body,
        (jnp.full((1, TQ), -jnp.inf, jnp.float32), jnp.zeros((1, TQ), jnp.float32),
         jnp.zeros((HEAD_DIM, TQ), jnp.float32)))
    result = (acc / total).astype(jnp.bfloat16)
    for copy in range(out.shape[1]):
        out[0, copy] = result


def attention(qkv, segment_ids, copies):
    tiles, _, chunk = qkv.shape
    count = tiles * chunk
    edges = segment_ids.reshape(count // TK, TK)
    key_low, key_high = edges[:, 0], edges[:, -1]
    query_edges = segment_ids.reshape(count // TQ, TQ)
    query_low, query_high = query_edges[:, 0], query_edges[:, -1]
    first = jnp.sum(key_high[None, :] < query_low[:, None], axis=1)
    last = jnp.sum(key_low[None, :] <= query_high[:, None], axis=1)
    bounds = jnp.stack([first, last]).astype(jnp.int32)
    per = chunk // TQ
    return pl.pallas_call(
        attention_kernel,
        out_shape=jax.ShapeDtypeStruct((tiles, copies, HEAD_DIM, chunk), jnp.bfloat16),
        grid_spec=pltpu.PrefetchScalarGridSpec(
            num_scalar_prefetch=1,
            grid=(count // TQ,),
            in_specs=[
                pl.BlockSpec(qkv.shape, lambda i, b: (0, 0, 0)),
                pl.BlockSpec((count, 1), lambda i, b: (0, 0)),
                pl.BlockSpec((1, count), lambda i, b: (0, 0)),
            ],
            out_specs=pl.BlockSpec((1, copies, HEAD_DIM, TQ), lambda i, b: (i // per, 0, 0, i % per)),
            scratch_shapes=[pltpu.VMEM((count, HEAD_DIM), jnp.bfloat16), pltpu.VMEM((count, 128), jnp.int32)],
        ),
        name="attention",
    )(bounds, qkv, segment_ids[:, None], segment_ids[None, :])


def per_device(tokens, segment_ids, w_qkv, w_out, w_merge, gain_attn, gain_merge):
    rows, cols = lax.axis_size("y"), lax.axis_size("x")
    tok_local = tokens.shape[0]
    core = lax.axis_index("c")
    half = D // 2
    weights = w_qkv.T
    own_qkv = lax.dynamic_slice_in_dim(weights, core * half, half, 1)
    mine_qkv = jnp.stack([shift_rows(own_qkv, step, rows) for step in (3, 2, 1)])
    row_tokens = broadcast_a2a(tokens, "x", cols).reshape(cols * tok_local, D)
    other_qkv = swap_cores(mine_qkv)
    residual = row_tokens.astype(jnp.float32)
    normed = layer_norm(residual, gain_attn).astype(jnp.bfloat16)
    normed_mine = lax.dynamic_slice_in_dim(normed, core * half, half, 1)
    normed_other = lax.dynamic_slice_in_dim(normed, (1 - core) * half, half, 1)
    own_heads = jnp.einsum("ck,tk->ct", weights, normed, preferred_element_type=jnp.float32)
    heads = (
        jnp.einsum("yck,tk->yct", mine_qkv, normed_mine, preferred_element_type=jnp.float32)
        + jnp.einsum("yck,tk->yct", other_qkv, normed_other, preferred_element_type=jnp.float32)
    )
    ahead = jnp.concatenate([own_heads[None], heads], axis=0).astype(jnp.bfloat16)
    me = lax.axis_index("y")
    qkv = lax.dynamic_slice_in_dim(jnp.concatenate([ahead, ahead], axis=0), (rows - me) % rows, rows, 0)
    by_head = lax.all_to_all(qkv, "y", split_axis=0, concat_axis=0, tiled=True)
    own_out = lax.dynamic_slice_in_dim(w_out, core * half, half, 1)
    mine_out = broadcast_a2a(own_out, ("y", "x"), rows * cols).reshape(D, half)
    other_out = swap_cores(mine_out)
    half_merge = w_merge.shape[0] // 2
    own_merge = lax.dynamic_slice_in_dim(w_merge, core * half_merge, half_merge, 0)
    own_merge, row_tokens = lax.optimization_barrier((own_merge, row_tokens))
    mine_merge = [shift_rows(own_merge, step, rows) for step in (1, 3, 2)]
    other_merge = [swap_cores(part) for part in mine_merge]

    attended = attention(by_head, segment_ids, cols)
    back = lax.all_to_all(
        attended.reshape(rows * cols, HEAD_DIM, cols * tok_local), ("y", "x"),
        split_axis=0, concat_axis=0, tiled=True).reshape(D, cols * tok_local)
    low_out = jnp.where(core == 0, mine_out, other_out)
    high_out = jnp.where(core == 0, other_out, mine_out)
    full_out = jnp.concatenate([low_out, high_out], axis=1)
    hidden = residual + jnp.einsum("kt,kd->td", back, full_out, preferred_element_type=jnp.float32)
    normed_two = layer_norm(hidden, gain_merge).astype(jnp.bfloat16)
    merged = normed_two.reshape(cols * tok_local // 4, 4 * D)
    merged_mine = lax.dynamic_slice_in_dim(merged, core * half_merge, half_merge, 1)
    merged_other = lax.dynamic_slice_in_dim(merged, (1 - core) * half_merge, half_merge, 1)
    blocks = [jnp.dot(merged, w_merge, preferred_element_type=jnp.float32)]
    for mine, other in zip(mine_merge, other_merge):
        blocks.append(
            jnp.dot(merged_mine, mine, preferred_element_type=jnp.float32)
            + jnp.dot(merged_other, other, preferred_element_type=jnp.float32))
    block = jnp.concatenate([part.astype(jnp.bfloat16) for part in blocks], axis=1)
    width = w_merge.shape[1]
    sent = block.reshape(cols, tok_local // 4, rows * width)
    got = lax.all_to_all(sent, "x", split_axis=0, concat_axis=0, tiled=True)
    got = got.reshape(cols, tok_local // 4, rows, width)
    placed = jnp.zeros((tok_local // 4, rows, cols, width), jnp.bfloat16)
    for index, back_by in enumerate((0, 1, 3, 2)):
        part = got[:, :, index, :].transpose(1, 0, 2)[:, None]
        placed = lax.dynamic_update_slice(placed, part, (0, (me + rows - back_by) % rows, 0, 0))
    return placed.reshape(tok_local // 4, rows * cols * width)


def solution(mesh):
    torus = Mesh(mesh.devices.reshape(mesh.shape["dp"] // 2, 2, 4, 4), ("z", "c", "y", "x"))
    dp, seq, both = ("z", "c"), ("y", "x"), ("z", "c", "y", "x")
    in_specs = (P(both, None), P(dp), P(None, seq), P(seq, None), P(None, seq), P(), P())
    return jax.shard_map(
        per_device, mesh=torus, in_specs=in_specs, out_specs=P(both, None), check_vma=False
    )
```

```python
import jax
import jax.numpy as jnp
from jax import lax
from jax.experimental import pallas as pl
from jax.experimental.pallas import tpu as pltpu
from jax.sharding import Mesh
from jax.sharding import PartitionSpec as P


D = 1280
HEADS = 16
HEAD_DIM = 80
TQ = 512
TK = 512
LOG2E = 1.4426950408889634


def layer_norm(vector, scale_gain):
    average = jnp.mean(vector, axis=-1, keepdims=True)
    centred = vector - average
    spread_sq = jnp.mean(centred * centred, axis=-1, keepdims=True)
    return centred * lax.rsqrt(spread_sq + 1e-06) * scale_gain


def swap_cores(value):
    return lax.ppermute(value, "c", [(0, 1), (1, 0)])


def shift_rows(value, step, rows):
    return lax.ppermute(value, "y", [(at, (at + step) % rows) for at in range(rows)])


def attention_kernel(bounds, qkv, seg_col, seg_row, out, keys, seg_wide):
    tiles, _, chunk = qkv.shape
    step = pl.program_id(0)
    per_chunk = chunk // TK

    @pl.when(step == 0)
    def _():
        for index in range(tiles):
            keys[index * chunk:(index + 1) * chunk, :] = qkv[index, HEAD_DIM:2 * HEAD_DIM, :].T
        seg_wide[...] = jnp.broadcast_to(seg_col[...], seg_wide.shape)

    part = step // (chunk // TQ)
    offset = pl.multiple_of((step % (chunk // TQ)) * TQ, TQ)
    queries = qkv[part, 0:HEAD_DIM, pl.ds(offset, TQ)]
    query_seg = seg_row[0:1, pl.ds(pl.multiple_of(step * TQ, TQ), TQ)]
    factor = (HEAD_DIM ** -0.5) * LOG2E

    def body(tile, carry):
        top, total, acc = carry
        start = pl.multiple_of(tile * TK, TK)
        scores = lax.dot_general(
            keys[pl.ds(start, TK), :], queries, (((1,), (0,)), ((), ())),
            preferred_element_type=jnp.float32)
        wide = seg_wide[pl.ds(start, TK), :]
        same = jnp.concatenate([wide] * (TQ // 128), axis=1) == query_seg
        scores = jnp.where(same, scores, -jnp.inf)
        new_top = jnp.maximum(top, jnp.max(scores, axis=0, keepdims=True))
        safe = jnp.where(new_top == -jnp.inf, 0.0, new_top)
        decay = jnp.exp2((top - safe) * factor)
        expo = jnp.exp2((scores - safe) * factor)
        total = total * decay + jnp.sum(expo, axis=0, keepdims=True)
        values = qkv[tile // per_chunk, 2 * HEAD_DIM:3 * HEAD_DIM,
                     pl.ds(pl.multiple_of((tile % per_chunk) * TK, TK), TK)]
        acc = acc * decay + lax.dot_general(
            values, expo.astype(jnp.bfloat16), (((1,), (0,)), ((), ())),
            preferred_element_type=jnp.float32)
        return new_top, total, acc

    first, last = bounds[0, step], bounds[1, step]
    _, total, acc = lax.fori_loop(
        first, last, body,
        (jnp.full((1, TQ), -jnp.inf, jnp.float32), jnp.zeros((1, TQ), jnp.float32),
         jnp.zeros((HEAD_DIM, TQ), jnp.float32)))
    result = (acc / total).astype(jnp.bfloat16)
    for copy in range(out.shape[1]):
        out[0, copy] = result


def attention(qkv, segments, segment_ids, copies):
    tiles, _, chunk = qkv.shape
    count = tiles * chunk
    edges = segment_ids.reshape(count // TK, TK)
    key_low, key_high = edges[:, 0], edges[:, -1]
    query_edges = segment_ids.reshape(count // TQ, TQ)
    query_low, query_high = query_edges[:, 0], query_edges[:, -1]
    first = jnp.sum(key_high[None, :] < query_low[:, None], axis=1)
    last = jnp.sum(key_low[None, :] <= query_high[:, None], axis=1)
    bounds = jnp.stack([first, last]).astype(jnp.int32)
    per = chunk // TQ
    return pl.pallas_call(
        attention_kernel,
        out_shape=jax.ShapeDtypeStruct((tiles, copies, HEAD_DIM, chunk), jnp.bfloat16),
        grid_spec=pltpu.PrefetchScalarGridSpec(
            num_scalar_prefetch=1,
            grid=(count // TQ,),
            in_specs=[
                pl.BlockSpec(qkv.shape, lambda i, b: (0, 0, 0)),
                pl.BlockSpec((count, 1), lambda i, b: (0, 0)),
                pl.BlockSpec((1, count), lambda i, b: (0, 0)),
            ],
            out_specs=pl.BlockSpec((1, copies, HEAD_DIM, TQ), lambda i, b: (i // per, 0, 0, i % per)),
            scratch_shapes=[pltpu.VMEM((count, HEAD_DIM), jnp.bfloat16), pltpu.VMEM((count, 128), jnp.int32)],
        ),
        name="attention",
    )(bounds, qkv, segments[:, None], segments[None, :])


def shift_cols(value, step, cols):
    return lax.ppermute(value, "x", [(at, (at + step) % cols) for at in range(cols)])


def shift_planes(value, step, planes):
    return lax.ppermute(value, "z", [(at, (at + step) % planes) for at in range(planes)])


def matmul(left, right, left_dim, right_dim):
    return lax.dot_general(
        left, right, (((left_dim,), (right_dim,)), ((), ())), preferred_element_type=jnp.float32)


def whole(shape):
    return pl.BlockSpec(shape, lambda *_: (0,) * len(shape))


def spread_kernel(tokens, out, wide):
    copies, count, _ = out.shape
    group = count // 4
    for lane in range(wide.shape[0]):
        wide[lane] = tokens[:, lane * 128:(lane + 1) * 128].astype(jnp.float32)
        for spot in range(4):
            part = wide[lane, pl.ds(spot, group, stride=4), :].astype(jnp.bfloat16)
            for copy in range(copies):
                out[copy, spot * group:(spot + 1) * group, lane * 128:(lane + 1) * 128] = part


def spread_tokens(tokens, copies):
    count, width = tokens.shape
    return pl.pallas_call(
        spread_kernel,
        out_shape=jax.ShapeDtypeStruct((copies, count, width), jnp.bfloat16),
        grid=(1,),
        in_specs=[whole(tokens.shape)],
        out_specs=whole((copies, count, width)),
        scratch_shapes=[pltpu.VMEM((width // 128, count, 128), jnp.float32)],
        name="spread",
    )(tokens)


def qkv_kernel(place, tokens, gain, own, first, second, third, other, out, normed):
    row, core = place[0], place[1]
    rows, wide, _ = out.shape
    half = D // 2
    count = normed.shape[0]
    value = layer_norm(tokens[...].reshape(count, D).astype(jnp.float32), gain[...])
    normed[...] = value.astype(jnp.bfloat16)
    out[row] = matmul(own[...], normed[...], 1, 1).astype(jnp.bfloat16)
    mine = normed[:, pl.ds(pl.multiple_of(core * half, half), half)]
    rest = normed[:, pl.ds(pl.multiple_of((1 - core) * half, half), half)]
    for index, part in enumerate((first, second, third)):
        value = matmul(part[0:wide, :], mine, 1, 1) + matmul(other[index], rest, 1, 1)
        out[(row + 1 + index) % rows] = value.astype(jnp.bfloat16)


def project_qkv(place, row_tokens, gain, weights, parts, other, rows):
    cols, count, _ = row_tokens.shape
    wide = weights.shape[0]
    return pl.pallas_call(
        qkv_kernel,
        out_shape=jax.ShapeDtypeStruct((rows, wide, cols * count), jnp.bfloat16),
        grid_spec=pltpu.PrefetchScalarGridSpec(
            num_scalar_prefetch=1,
            grid=(cols // 2,),
            in_specs=[pl.BlockSpec((2, count, D), lambda i, p: (i, 0, 0)), whole((1, D)), whole(weights.shape)]
            + [whole(part.shape) for part in parts] + [whole(other.shape)],
            out_specs=pl.BlockSpec((rows, wide, 2 * count), lambda i, p: (0, 0, i)),
            scratch_shapes=[pltpu.VMEM((2 * count, D), jnp.bfloat16)],
        ),
        name="project_qkv",
    )(place, row_tokens, gain[None], weights, *parts, other)


def hidden_kernel(place, back, residual, mine, other, gain, out, left, hidden):
    row, col, core = place[0], place[1], place[2]
    cols, rows = mine.shape[0], mine.shape[1]
    half = D // 2
    count = hidden.shape[0]
    for at_col in range(cols):
        for at_row in range(rows):
            head = ((row + at_row) % rows) * cols + (col + cols - at_col) % cols
            at = (at_col * rows + at_row) * HEAD_DIM
            left[at:at + HEAD_DIM, :] = back[head]
    turned = left[...].T
    hidden[:, pl.ds(pl.multiple_of(core * half, half), half)] = matmul(turned, mine[...].reshape(D, half), 1, 0)
    hidden[:, pl.ds(pl.multiple_of((1 - core) * half, half), half)] = matmul(
        turned, other[...].reshape(D, half), 1, 0)
    total = residual[...].reshape(count, D).astype(jnp.float32) + hidden[...]
    value = layer_norm(total, gain[...]).astype(jnp.bfloat16)
    group = count // 4
    for spot in range(4):
        out[spot, 0] = value[spot * group:(spot + 1) * group, :]


def merge_rows(place, back, row_tokens, mine, other, gain):
    cols, count, _ = row_tokens.shape
    return pl.pallas_call(
        hidden_kernel,
        out_shape=jax.ShapeDtypeStruct((4, cols, count // 4, D), jnp.bfloat16),
        grid_spec=pltpu.PrefetchScalarGridSpec(
            num_scalar_prefetch=1,
            grid=(cols,),
            in_specs=[
                pl.BlockSpec((HEADS, HEAD_DIM, count), lambda i, p: (0, 0, i)),
                pl.BlockSpec((1, count, D), lambda i, p: (i, 0, 0)),
                whole(mine.shape), whole(other.shape), whole((1, D)),
            ],
            out_specs=pl.BlockSpec((4, 1, count // 4, D), lambda i, p: (0, i, 0, 0)),
            scratch_shapes=[pltpu.VMEM((D, count), jnp.bfloat16), pltpu.VMEM((count, D), jnp.float32)],
        ),
        name="merge_rows",
    )(place, back, row_tokens, mine, other, gain[None])


def merge_kernel(order, rows, own, *rest):
    parts, out = rest[:-1], rest[-1]
    width = own.shape[1]
    total = matmul(rows[0], own[0:D, :], 1, 0)
    for spot in range(1, 4):
        total = total + matmul(rows[spot], own[spot * D:(spot + 1) * D, :], 1, 0)
    out[:, 0:width] = total.astype(jnp.bfloat16)
    for block in range(len(parts) // 4):
        total = matmul(rows[order[0]], parts[4 * block][...], 1, 0)
        for index in range(1, 4):
            total = total + matmul(rows[order[index]], parts[4 * block + index][...], 1, 0)
        out[:, (block + 1) * width:(block + 2) * width] = total.astype(jnp.bfloat16)


def merge(order, rows, own, parts):
    width = own.shape[1] * (1 + len(parts) // 4)
    return pl.pallas_call(
        merge_kernel,
        out_shape=jax.ShapeDtypeStruct((rows.shape[1], width), jnp.bfloat16),
        grid_spec=pltpu.PrefetchScalarGridSpec(
            num_scalar_prefetch=1,
            grid=(1,),
            in_specs=[whole(rows.shape), whole(own.shape)] + [whole(part.shape) for part in parts],
            out_specs=whole((rows.shape[1], width)),
        ),
        name="merge",
    )(order, rows, own, *parts)


BACK_BY = (0, 1, 3, 2)


def place_kernel(place, got, out):
    cols, _, wide = got.shape
    rows = len(BACK_BY)
    width = wide // rows
    for at_col in range(cols):
        for index, back_by in enumerate(BACK_BY):
            at = (((place[0] + rows - back_by) % rows) * cols + at_col) * width
            out[:, pl.ds(pl.multiple_of(at, width), width)] = got[at_col, :, index * width:(index + 1) * width]


def place_columns(place, got):
    cols, count, wide = got.shape
    return pl.pallas_call(
        place_kernel,
        out_shape=jax.ShapeDtypeStruct((count, cols * wide), jnp.bfloat16),
        grid_spec=pltpu.PrefetchScalarGridSpec(
            num_scalar_prefetch=1, grid=(1,), in_specs=[whole(got.shape)],
            out_specs=whole((count, cols * wide))),
        name="place_columns",
    )(place, got)


def block_step(tokens, segment_ids, w_qkv, w_out, w_merge, gain_attn, gain_merge):
    rows, cols, planes = lax.axis_size("y"), lax.axis_size("x"), lax.axis_size("z")
    row, col, core = lax.axis_index("y"), lax.axis_index("x"), lax.axis_index("c")
    parity = lax.axis_index("z") % 2
    tok_local = tokens.shape[0]
    groups = tok_local // 4
    row_count = cols * tok_local
    half = D // 2
    wide = w_qkv.shape[1]
    row_tokens = lax.all_to_all(
        spread_tokens(tokens, cols), "x", split_axis=0, concat_axis=0, tiled=True)
    segments = segment_ids.reshape(rows * cols, groups, 4).transpose(0, 2, 1).reshape(-1)

    weights = w_qkv.T
    own = jnp.concatenate([
        lax.dynamic_slice_in_dim(weights, core * half, half, 1),
        lax.dynamic_slice_in_dim(w_out, core * half, half, 1)], axis=0)
    ahead = [shift_rows(own, step, rows) for step in (3, 2, 1)]
    other_qkv = swap_cores(jnp.stack([part[:wide] for part in ahead]))

    order = [parity * 2 + core, (1 - parity) * 2 + core, parity * 2 + 1 - core, (1 - parity) * 2 + 1 - core]
    own_piece = lax.dynamic_slice_in_dim(w_merge, order[0] * D, D, 0)
    first_y = shift_rows(own_piece, 1, rows)
    third_y = shift_rows(own_piece, 3, rows)

    qkv = project_qkv(
        jnp.stack([row, core]).astype(jnp.int32), row_tokens, gain_attn, weights, ahead, other_qkv, rows)
    by_head = lax.all_to_all(qkv, "y", split_axis=0, concat_axis=0, tiled=True)

    out_rows = jnp.stack([own[wide:]] + [part[wide:] for part in ahead])
    out_parts = [out_rows] + [shift_cols(out_rows, step, cols) for step in (1, 2, 3)]
    first_z = shift_planes(first_y, 1, planes)
    third_z = shift_planes(third_y, planes - 1, planes)
    second_y = shift_rows(own_piece, 2, rows)

    attended = attention(by_head, segments, segment_ids, cols)
    back = lax.all_to_all(
        attended.reshape(rows * cols, HEAD_DIM, row_count), ("y", "x"),
        split_axis=0, concat_axis=0, tiled=True)
    second_z = shift_planes(second_y, 1, planes)
    mine_out = jnp.stack(out_parts)
    other_out = swap_cores(mine_out)
    parts = []
    for part_y, part_z in ((first_y, first_z), (third_y, third_z)):
        parts += [part_y, part_z, swap_cores(part_y), swap_cores(part_z)]
    parts += [second_y, second_z, swap_cores(second_y), swap_cores(second_z)]

    merged = merge_rows(
        jnp.stack([row, col, core]).astype(jnp.int32), back, row_tokens, mine_out, other_out, gain_merge)
    block = merge(
        jnp.stack(order).astype(jnp.int32), merged.reshape(4, cols * groups, D), w_merge, parts)
    got = lax.all_to_all(
        block.reshape(cols, groups, block.shape[1]), "x", split_axis=0, concat_axis=0, tiled=True)
    return place_columns(row[None].astype(jnp.int32), got)


def solution(mesh):
    torus = Mesh(mesh.devices.reshape(mesh.shape["dp"] // 2, 2, 4, 4), ("z", "c", "y", "x"))
    dp, seq, both = ("z", "c"), ("y", "x"), ("z", "c", "y", "x")
    in_specs = (P(both, None), P(dp), P(None, seq), P(seq, None), P(None, seq), P(), P())
    return jax.shard_map(block_step, mesh=torus, in_specs=in_specs, out_specs=P(both, None), check_vma=False)
```

```python
import jax
import jax.numpy as jnp
from jax import lax
from jax.experimental import pallas as pl
from jax.experimental.pallas import tpu as pltpu
from jax.sharding import Mesh
from jax.sharding import PartitionSpec as P


D = 1280
HEADS = 16
HEAD_DIM = 80
TQ = 512
TK = 512
LOG2E = 1.4426950408889634


def layer_norm(vector, scale_gain):
    average = jnp.mean(vector, axis=-1, keepdims=True)
    centred = vector - average
    spread_sq = jnp.mean(centred * centred, axis=-1, keepdims=True)
    return centred * lax.rsqrt(spread_sq + 1e-06) * scale_gain


def swap_cores(value):
    return lax.ppermute(value, "c", [(0, 1), (1, 0)])


def shift_rows(value, step, rows):
    return lax.ppermute(value, "y", [(at, (at + step) % rows) for at in range(rows)])


def attention_kernel(bounds, qkv, seg_col, seg_row, out, keys, seg_wide):
    tiles, _, chunk = qkv.shape
    step = pl.program_id(0)
    per_chunk = chunk // TK

    @pl.when(step == 0)
    def _():
        for index in range(tiles):
            keys[index * chunk:(index + 1) * chunk, :] = qkv[index, HEAD_DIM:2 * HEAD_DIM, :].T
        seg_wide[...] = jnp.broadcast_to(seg_col[...], seg_wide.shape)

    part = step // (chunk // TQ)
    offset = pl.multiple_of((step % (chunk // TQ)) * TQ, TQ)
    queries = qkv[part, 0:HEAD_DIM, pl.ds(offset, TQ)]
    query_seg = seg_row[0:1, pl.ds(pl.multiple_of(step * TQ, TQ), TQ)]
    factor = (HEAD_DIM ** -0.5) * LOG2E

    def body(tile, carry):
        top, total, acc = carry
        start = pl.multiple_of(tile * TK, TK)
        scores = lax.dot_general(
            keys[pl.ds(start, TK), :], queries, (((1,), (0,)), ((), ())),
            preferred_element_type=jnp.float32)
        wide = seg_wide[pl.ds(start, TK), :]
        same = jnp.concatenate([wide] * (TQ // 128), axis=1) == query_seg
        scores = jnp.where(same, scores, -jnp.inf)
        new_top = jnp.maximum(top, jnp.max(scores, axis=0, keepdims=True))
        safe = jnp.where(new_top == -jnp.inf, 0.0, new_top)
        decay = jnp.exp2((top - safe) * factor)
        expo = jnp.exp2((scores - safe) * factor)
        total = total * decay + jnp.sum(expo, axis=0, keepdims=True)
        values = qkv[tile // per_chunk, 2 * HEAD_DIM:3 * HEAD_DIM,
                     pl.ds(pl.multiple_of((tile % per_chunk) * TK, TK), TK)]
        acc = acc * decay + lax.dot_general(
            values, expo.astype(jnp.bfloat16), (((1,), (0,)), ((), ())),
            preferred_element_type=jnp.float32)
        return new_top, total, acc

    first, last = bounds[0, step], bounds[1, step]
    _, total, acc = lax.fori_loop(
        first, last, body,
        (jnp.full((1, TQ), -jnp.inf, jnp.float32), jnp.zeros((1, TQ), jnp.float32),
         jnp.zeros((HEAD_DIM, TQ), jnp.float32)))
    result = (acc / total).astype(jnp.bfloat16)
    for copy in range(out.shape[1]):
        out[0, copy] = result


def attention_inputs(segments, segment_ids):
    edges = segment_ids.reshape(-1, TK)
    key_low, key_high = edges[:, 0], edges[:, -1]
    query_edges = segment_ids.reshape(-1, TQ)
    query_low, query_high = query_edges[:, 0], query_edges[:, -1]
    first = jnp.sum(key_high[None, :] < query_low[:, None], axis=1)
    last = jnp.sum(key_low[None, :] <= query_high[:, None], axis=1)
    bounds = jnp.stack([first, last]).astype(jnp.int32)
    return bounds, segments[:, None], segments[None, :]


def attention(qkv, layout, copies):
    tiles, _, chunk = qkv.shape
    count = tiles * chunk
    bounds, seg_col, seg_row = layout
    per = chunk // TQ
    return pl.pallas_call(
        attention_kernel,
        out_shape=jax.ShapeDtypeStruct((tiles, copies, HEAD_DIM, chunk), jnp.bfloat16),
        grid_spec=pltpu.PrefetchScalarGridSpec(
            num_scalar_prefetch=1,
            grid=(count // TQ,),
            in_specs=[
                pl.BlockSpec(qkv.shape, lambda i, b: (0, 0, 0)),
                pl.BlockSpec((count, 1), lambda i, b: (0, 0)),
                pl.BlockSpec((1, count), lambda i, b: (0, 0)),
            ],
            out_specs=pl.BlockSpec((1, copies, HEAD_DIM, TQ), lambda i, b: (i // per, 0, 0, i % per)),
            scratch_shapes=[pltpu.VMEM((count, HEAD_DIM), jnp.bfloat16), pltpu.VMEM((count, 128), jnp.int32)],
        ),
        name="attention",
    )(bounds, qkv, seg_col, seg_row)


def shift_cols(value, step, cols):
    return lax.ppermute(value, "x", [(at, (at + step) % cols) for at in range(cols)])


def shift_planes(value, step, planes):
    return lax.ppermute(value, "z", [(at, (at + step) % planes) for at in range(planes)])


def matmul(left, right, left_dim, right_dim):
    return lax.dot_general(
        left, right, (((left_dim,), (right_dim,)), ((), ())), preferred_element_type=jnp.float32)


def whole(shape):
    return pl.BlockSpec(shape, lambda *_: (0,) * len(shape))


def spread_kernel(tokens, out, wide):
    copies, count, _ = out.shape
    group = count // 4
    for lane in range(wide.shape[0]):
        wide[lane] = tokens[:, lane * 128:(lane + 1) * 128].astype(jnp.float32)
        for spot in range(4):
            part = wide[lane, pl.ds(spot, group, stride=4), :].astype(jnp.bfloat16)
            for copy in range(copies):
                out[copy, spot * group:(spot + 1) * group, lane * 128:(lane + 1) * 128] = part


def spread_tokens(tokens, copies):
    count, width = tokens.shape
    return pl.pallas_call(
        spread_kernel,
        out_shape=jax.ShapeDtypeStruct((copies, count, width), jnp.bfloat16),
        grid=(1,),
        in_specs=[whole(tokens.shape)],
        out_specs=whole((copies, count, width)),
        scratch_shapes=[pltpu.VMEM((width // 128, count, 128), jnp.float32)],
        name="spread",
    )(tokens)


def qkv_kernel(place, tokens, gain, own, first, second, third, other, out, normed):
    row, core = place[0], place[1]
    rows, wide, _ = out.shape
    half = D // 2
    count = normed.shape[0]
    value = layer_norm(tokens[...].reshape(count, D).astype(jnp.float32), gain[...])
    normed[...] = value.astype(jnp.bfloat16)
    out[row] = matmul(own[...], normed[...], 1, 1).astype(jnp.bfloat16)
    mine = normed[:, pl.ds(pl.multiple_of(core * half, half), half)]
    rest = normed[:, pl.ds(pl.multiple_of((1 - core) * half, half), half)]
    for index, part in enumerate((first, second, third)):
        value = matmul(part[0:wide, :], mine, 1, 1) + matmul(other[index], rest, 1, 1)
        out[(row + 1 + index) % rows] = value.astype(jnp.bfloat16)


def project_qkv(place, row_tokens, gain, weights, parts, other, rows):
    cols, count, _ = row_tokens.shape
    wide = weights.shape[0]
    return pl.pallas_call(
        qkv_kernel,
        out_shape=jax.ShapeDtypeStruct((rows, wide, cols * count), jnp.bfloat16),
        grid_spec=pltpu.PrefetchScalarGridSpec(
            num_scalar_prefetch=1,
            grid=(cols // 2,),
            in_specs=[pl.BlockSpec((2, count, D), lambda i, p: (i, 0, 0)), whole((D,)), whole(weights.shape)]
            + [whole(part.shape) for part in parts] + [whole(other.shape)],
            out_specs=pl.BlockSpec((rows, wide, 2 * count), lambda i, p: (0, 0, i)),
            scratch_shapes=[pltpu.VMEM((2 * count, D), jnp.bfloat16)],
        ),
        name="project_qkv",
    )(place, row_tokens, gain, weights, *parts, other)


def hidden_kernel(place, back, residual, mine, other, gain, out, left, hidden):
    row, core, col = place[0], place[1], place[2]
    cols, rows = mine.shape[0], mine.shape[1]
    half = D // 2
    count = hidden.shape[0]
    for at_col in range(cols):
        for at_row in range(rows):
            head = ((row + at_row) % rows) * cols + (col + cols - at_col) % cols
            at = (at_col * rows + at_row) * HEAD_DIM
            left[at:at + HEAD_DIM, :] = back[head]
    turned = left[...].T
    hidden[:, pl.ds(pl.multiple_of(core * half, half), half)] = matmul(turned, mine[...].reshape(D, half), 1, 0)
    hidden[:, pl.ds(pl.multiple_of((1 - core) * half, half), half)] = matmul(
        turned, other[...].reshape(D, half), 1, 0)
    total = residual[...].reshape(count, D).astype(jnp.float32) + hidden[...]
    value = layer_norm(total, gain[...]).astype(jnp.bfloat16)
    group = count // 4
    for spot in range(4):
        out[spot, 0] = value[spot * group:(spot + 1) * group, :]


def merge_rows(place, back, row_tokens, mine, other, gain):
    cols, count, _ = row_tokens.shape
    return pl.pallas_call(
        hidden_kernel,
        out_shape=jax.ShapeDtypeStruct((4, cols, count // 4, D), jnp.bfloat16),
        grid_spec=pltpu.PrefetchScalarGridSpec(
            num_scalar_prefetch=1,
            grid=(cols,),
            in_specs=[
                pl.BlockSpec((HEADS, HEAD_DIM, count), lambda i, p: (0, 0, i)),
                pl.BlockSpec((1, count, D), lambda i, p: (i, 0, 0)),
                whole(mine.shape), whole(other.shape), whole((D,)),
            ],
            out_specs=pl.BlockSpec((4, 1, count // 4, D), lambda i, p: (0, i, 0, 0)),
            scratch_shapes=[pltpu.VMEM((D, count), jnp.bfloat16), pltpu.VMEM((count, D), jnp.float32)],
        ),
        name="merge_rows",
    )(place, back, row_tokens, mine, other, gain)


def merge_kernel(place, rows, own, *rest):
    parts, out = rest[:-1], rest[-1]
    core, parity = place[1], place[3]
    order = (parity * 2 + core, 2 - parity * 2 + core, parity * 2 + 1 - core, 3 - parity * 2 - core)
    width = own.shape[1]
    total = matmul(rows[0], own[0:D, :], 1, 0)
    for spot in range(1, 4):
        total = total + matmul(rows[spot], own[spot * D:(spot + 1) * D, :], 1, 0)
    out[:, 0:width] = total.astype(jnp.bfloat16)
    for block in range(len(parts) // 4):
        total = matmul(rows[order[0]], parts[4 * block][...], 1, 0)
        for index in range(1, 4):
            total = total + matmul(rows[order[index]], parts[4 * block + index][...], 1, 0)
        out[:, (block + 1) * width:(block + 2) * width] = total.astype(jnp.bfloat16)


def merge(place, rows, own, parts):
    width = own.shape[1] * (1 + len(parts) // 4)
    return pl.pallas_call(
        merge_kernel,
        out_shape=jax.ShapeDtypeStruct((rows.shape[1], width), jnp.bfloat16),
        grid_spec=pltpu.PrefetchScalarGridSpec(
            num_scalar_prefetch=1,
            grid=(1,),
            in_specs=[whole(rows.shape), whole(own.shape)] + [whole(part.shape) for part in parts],
            out_specs=whole((rows.shape[1], width)),
        ),
        name="merge",
    )(place, rows, own, *parts)


BACK_BY = (0, 1, 3, 2)


def place_kernel(place, got, out):
    cols, _, wide = got.shape
    rows = len(BACK_BY)
    width = wide // rows
    for at_col in range(cols):
        for index, back_by in enumerate(BACK_BY):
            at = (((place[0] + rows - back_by) % rows) * cols + at_col) * width
            out[:, pl.ds(pl.multiple_of(at, width), width)] = got[at_col, :, index * width:(index + 1) * width]


def place_columns(place, got):
    cols, count, wide = got.shape
    return pl.pallas_call(
        place_kernel,
        out_shape=jax.ShapeDtypeStruct((count, cols * wide), jnp.bfloat16),
        grid_spec=pltpu.PrefetchScalarGridSpec(
            num_scalar_prefetch=1, grid=(1,), in_specs=[whole(got.shape)],
            out_specs=whole((count, cols * wide))),
        name="place_columns",
    )(place, got)


def block_step(tokens, segment_ids, w_qkv, w_out, w_merge, gain_attn, gain_merge):
    rows, cols, planes = lax.axis_size("y"), lax.axis_size("x"), lax.axis_size("z")
    row, col, core = lax.axis_index("y"), lax.axis_index("x"), lax.axis_index("c")
    parity = lax.axis_index("z") % 2
    tok_local = tokens.shape[0]
    groups = tok_local // 4
    row_count = cols * tok_local
    half = D // 2
    wide = w_qkv.shape[1]
    place = jnp.stack([row, core, col, parity]).astype(jnp.int32)
    segments = segment_ids.reshape(rows * cols, groups, 4).transpose(0, 2, 1).reshape(-1)
    layout = attention_inputs(segments, segment_ids)
    row_tokens = lax.all_to_all(
        spread_tokens(tokens, cols), "x", split_axis=0, concat_axis=0, tiled=True)

    weights = w_qkv.T
    own = jnp.concatenate([
        lax.dynamic_slice_in_dim(weights, core * half, half, 1),
        lax.dynamic_slice_in_dim(w_out, core * half, half, 1)], axis=0)
    ahead = [shift_rows(own, step, rows) for step in (3, 2, 1)]
    other_qkv = swap_cores(jnp.stack([part[:wide] for part in ahead]))

    own_piece = lax.dynamic_slice_in_dim(w_merge, (parity * 2 + core) * D, D, 0)
    first_y = shift_rows(own_piece, 1, rows)
    third_y = shift_rows(own_piece, 3, rows)

    qkv = project_qkv(
        place, row_tokens, gain_attn, weights, ahead, other_qkv, rows)
    by_head = lax.all_to_all(qkv, "y", split_axis=0, concat_axis=0, tiled=True)

    out_rows = jnp.stack([own[wide:]] + [part[wide:] for part in ahead])
    next_out = shift_cols(out_rows, 1, cols)
    out_parts = [out_rows, next_out] + [shift_cols(out_rows, step, cols) for step in (2, 3)]
    first_z = shift_planes(first_y, 1, planes)
    third_z = shift_planes(third_y, planes - 1, planes)
    second_y = shift_rows(own_piece, 2, rows)

    attended = attention(by_head, layout, cols)
    back = lax.all_to_all(
        attended.reshape(rows * cols, HEAD_DIM, row_count), ("y", "x"),
        split_axis=0, concat_axis=0, tiled=True)
    second_z = shift_planes(second_y, 1, planes)
    mine_out = jnp.stack(out_parts)
    other_out = swap_cores(mine_out)
    parts = []
    for part_y, part_z in ((first_y, first_z), (third_y, third_z)):
        parts += [part_y, part_z, swap_cores(part_y), swap_cores(part_z)]
    parts += [second_y, second_z, swap_cores(second_y), swap_cores(second_z)]

    merged = merge_rows(
        place, back, row_tokens, mine_out, other_out, gain_merge)
    block = merge(
        place, merged.reshape(4, cols * groups, D), w_merge, parts)
    got = lax.all_to_all(
        block.reshape(cols, groups, block.shape[1]), "x", split_axis=0, concat_axis=0, tiled=True)
    return place_columns(place, got)


def solution(mesh):
    torus = Mesh(mesh.devices.reshape(mesh.shape["dp"] // 2, 2, 4, 4), ("z", "c", "y", "x"))
    dp, seq, both = ("z", "c"), ("y", "x"), ("z", "c", "y", "x")
    in_specs = (P(both, None), P(dp), P(None, seq), P(seq, None), P(None, seq), P(), P())
    return jax.shard_map(block_step, mesh=torus, in_specs=in_specs, out_specs=P(both, None), check_vma=False)
```

```python
import jax
import jax.numpy as jnp
from jax import lax
from jax.experimental import pallas as pl
from jax.experimental.pallas import tpu as pltpu
from jax.sharding import Mesh
from jax.sharding import PartitionSpec as P


D = 1280
HEADS = 16
HEAD_DIM = 80
TQ = 512
TK = 512
LOG2E = 1.4426950408889634


def layer_norm(vector, scale_gain):
    average = jnp.mean(vector, axis=-1, keepdims=True)
    centred = vector - average
    spread_sq = jnp.mean(centred * centred, axis=-1, keepdims=True)
    return centred * lax.rsqrt(spread_sq + 1e-06) * scale_gain


def swap_cores(value):
    return lax.ppermute(value, "c", [(0, 1), (1, 0)])


def shift_rows(value, step, rows):
    return lax.ppermute(value, "y", [(at, (at + step) % rows) for at in range(rows)])


def attention_kernel(bounds, qkv, seg_col, seg_row, out, keys, seg_wide):
    tiles, _, chunk = qkv.shape
    step = pl.program_id(0)
    per_chunk = chunk // TK

    @pl.when(step == 0)
    def _():
        for index in range(tiles):
            keys[index * chunk:(index + 1) * chunk, :] = qkv[index, HEAD_DIM:2 * HEAD_DIM, :].T
        seg_wide[...] = jnp.broadcast_to(seg_col[...], seg_wide.shape)

    part = step // (chunk // TQ)
    offset = pl.multiple_of((step % (chunk // TQ)) * TQ, TQ)
    queries = qkv[part, 0:HEAD_DIM, pl.ds(offset, TQ)]
    query_seg = seg_row[0:1, pl.ds(pl.multiple_of(step * TQ, TQ), TQ)]
    factor = (HEAD_DIM ** -0.5) * LOG2E

    def body(tile, carry):
        top, total, acc = carry
        start = pl.multiple_of(tile * TK, TK)
        scores = lax.dot_general(
            keys[pl.ds(start, TK), :], queries, (((1,), (0,)), ((), ())),
            preferred_element_type=jnp.float32)
        wide = seg_wide[pl.ds(start, TK), :]
        same = jnp.concatenate([wide] * (TQ // 128), axis=1) == query_seg
        scores = jnp.where(same, scores, -jnp.inf)
        new_top = jnp.maximum(top, jnp.max(scores, axis=0, keepdims=True))
        safe = jnp.where(new_top == -jnp.inf, 0.0, new_top)
        decay = jnp.exp2((top - safe) * factor)
        expo = jnp.exp2((scores - safe) * factor)
        total = total * decay + jnp.sum(expo, axis=0, keepdims=True)
        values = qkv[tile // per_chunk, 2 * HEAD_DIM:3 * HEAD_DIM,
                     pl.ds(pl.multiple_of((tile % per_chunk) * TK, TK), TK)]
        acc = acc * decay + lax.dot_general(
            values, expo.astype(jnp.bfloat16), (((1,), (0,)), ((), ())),
            preferred_element_type=jnp.float32)
        return new_top, total, acc

    first, last = bounds[0, step], bounds[1, step]
    _, total, acc = lax.fori_loop(
        first, last, body,
        (jnp.full((1, TQ), -jnp.inf, jnp.float32), jnp.zeros((1, TQ), jnp.float32),
         jnp.zeros((HEAD_DIM, TQ), jnp.float32)))
    result = (acc / total).astype(jnp.bfloat16)
    for copy in range(out.shape[1]):
        out[0, copy] = result


def attention_inputs(segments, segment_ids):
    edges = segment_ids.reshape(-1, TK)
    key_low, key_high = edges[:, 0], edges[:, -1]
    query_edges = segment_ids.reshape(-1, TQ)
    query_low, query_high = query_edges[:, 0], query_edges[:, -1]
    first = jnp.sum(key_high[None, :] < query_low[:, None], axis=1)
    last = jnp.sum(key_low[None, :] <= query_high[:, None], axis=1)
    bounds = jnp.stack([first, last]).astype(jnp.int32)
    return bounds, segments[:, None], segments[None, :]


def attention(qkv, layout, copies):
    tiles, _, chunk = qkv.shape
    count = tiles * chunk
    bounds, seg_col, seg_row = layout
    per = chunk // TQ
    return pl.pallas_call(
        attention_kernel,
        out_shape=jax.ShapeDtypeStruct((tiles, copies, HEAD_DIM, chunk), jnp.bfloat16),
        grid_spec=pltpu.PrefetchScalarGridSpec(
            num_scalar_prefetch=1,
            grid=(count // TQ,),
            in_specs=[
                pl.BlockSpec(qkv.shape, lambda i, b: (0, 0, 0)),
                pl.BlockSpec((count, 1), lambda i, b: (0, 0)),
                pl.BlockSpec((1, count), lambda i, b: (0, 0)),
            ],
            out_specs=pl.BlockSpec((1, copies, HEAD_DIM, TQ), lambda i, b: (i // per, 0, 0, i % per)),
            scratch_shapes=[pltpu.VMEM((count, HEAD_DIM), jnp.bfloat16), pltpu.VMEM((count, 128), jnp.int32)],
        ),
        name="attention",
    )(bounds, qkv, seg_col, seg_row)


def shift_cols(value, step, cols):
    return lax.ppermute(value, "x", [(at, (at + step) % cols) for at in range(cols)])


def shift_planes(value, step, planes):
    return lax.ppermute(value, "z", [(at, (at + step) % planes) for at in range(planes)])


def matmul(left, right, left_dim, right_dim):
    return lax.dot_general(
        left, right, (((left_dim,), (right_dim,)), ((), ())), preferred_element_type=jnp.float32)


def whole(shape):
    return pl.BlockSpec(shape, lambda *_: (0,) * len(shape))


def spread_kernel(tokens, out, wide):
    copies, count, _ = out.shape
    group = count // 4
    for lane in range(wide.shape[0]):
        wide[lane] = tokens[:, lane * 128:(lane + 1) * 128].astype(jnp.float32)
        for spot in range(4):
            part = wide[lane, pl.ds(spot, group, stride=4), :].astype(jnp.bfloat16)
            for copy in range(copies):
                out[copy, spot * group:(spot + 1) * group, lane * 128:(lane + 1) * 128] = part


def spread_tokens(tokens, copies):
    count, width = tokens.shape
    return pl.pallas_call(
        spread_kernel,
        out_shape=jax.ShapeDtypeStruct((copies, count, width), jnp.bfloat16),
        grid=(1,),
        in_specs=[whole(tokens.shape)],
        out_specs=whole((copies, count, width)),
        scratch_shapes=[pltpu.VMEM((width // 128, count, 128), jnp.float32)],
        name="spread",
    )(tokens)


def qkv_kernel(place, tokens, gain, own, first, second, third, other, out, normed):
    row, core = place[0], place[1]
    rows, wide, _ = out.shape
    half = D // 2
    count = normed.shape[0]
    value = layer_norm(tokens[...].reshape(count, D).astype(jnp.float32), gain[...])
    normed[...] = value.astype(jnp.bfloat16)
    out[row] = matmul(own[...], normed[...], 1, 1).astype(jnp.bfloat16)
    mine = normed[:, pl.ds(pl.multiple_of(core * half, half), half)]
    rest = normed[:, pl.ds(pl.multiple_of((1 - core) * half, half), half)]
    for index, part in enumerate((first, second, third)):
        value = matmul(part[0:wide, :], mine, 1, 1) + matmul(other[index], rest, 1, 1)
        out[(row + 1 + index) % rows] = value.astype(jnp.bfloat16)


def project_qkv(place, row_tokens, gain, weights, parts, other, rows):
    cols, count, _ = row_tokens.shape
    wide = weights.shape[0]
    return pl.pallas_call(
        qkv_kernel,
        out_shape=jax.ShapeDtypeStruct((rows, wide, cols * count), jnp.bfloat16),
        grid_spec=pltpu.PrefetchScalarGridSpec(
            num_scalar_prefetch=1,
            grid=(cols // 2,),
            in_specs=[pl.BlockSpec((2, count, D), lambda i, p: (i, 0, 0)), whole((D,)), whole(weights.shape)]
            + [whole(part.shape) for part in parts] + [whole(other.shape)],
            out_specs=pl.BlockSpec((rows, wide, 2 * count), lambda i, p: (0, 0, i)),
            scratch_shapes=[pltpu.VMEM((2 * count, D), jnp.bfloat16)],
        ),
        name="project_qkv",
    )(place, row_tokens, gain, weights, *parts, other)


def hidden_kernel(place, back, residual, mine, other, gain, out, left, hidden):
    row, core, col = place[0], place[1], place[2]
    cols, rows = mine.shape[0], mine.shape[1]
    half = D // 2
    count = hidden.shape[0]
    for at_col in range(cols):
        for at_row in range(rows):
            head = ((row + at_row) % rows) * cols + (col + cols - at_col) % cols
            at = (at_col * rows + at_row) * HEAD_DIM
            left[at:at + HEAD_DIM, :] = back[head]
    turned = left[...].T
    hidden[:, pl.ds(pl.multiple_of(core * half, half), half)] = matmul(turned, mine[...].reshape(D, half), 1, 0)
    hidden[:, pl.ds(pl.multiple_of((1 - core) * half, half), half)] = matmul(
        turned, other[...].reshape(D, half), 1, 0)
    total = residual[...].reshape(count, D).astype(jnp.float32) + hidden[...]
    value = layer_norm(total, gain[...]).astype(jnp.bfloat16)
    group = count // 4
    for spot in range(4):
        out[spot, 0] = value[spot * group:(spot + 1) * group, :]


def merge_rows(place, back, row_tokens, mine, other, gain):
    cols, count, _ = row_tokens.shape
    return pl.pallas_call(
        hidden_kernel,
        out_shape=jax.ShapeDtypeStruct((4, cols, count // 4, D), jnp.bfloat16),
        grid_spec=pltpu.PrefetchScalarGridSpec(
            num_scalar_prefetch=1,
            grid=(cols,),
            in_specs=[
                pl.BlockSpec((HEADS, HEAD_DIM, count), lambda i, p: (0, 0, i)),
                pl.BlockSpec((1, count, D), lambda i, p: (i, 0, 0)),
                whole(mine.shape), whole(other.shape), whole((D,)),
            ],
            out_specs=pl.BlockSpec((4, 1, count // 4, D), lambda i, p: (0, i, 0, 0)),
            scratch_shapes=[pltpu.VMEM((D, count), jnp.bfloat16), pltpu.VMEM((count, D), jnp.float32)],
        ),
        name="merge_rows",
    )(place, back, row_tokens, mine, other, gain)


def merge_kernel(place, mine, other, own, *rest):
    parts, out = rest[:-1], rest[-1]
    core, parity = place[1], place[3]
    lanes = parts[0].shape[1]
    column = pl.multiple_of(core * lanes, lanes)
    for source, target in ((mine, core), (other, 1 - core)):
        near = jnp.concatenate([source[parity * 2], source[parity * 2 + 1]], axis=1)
        far = jnp.concatenate([source[2 - parity * 2], source[3 - parity * 2]], axis=1)
        flat = jnp.concatenate([source[spot] for spot in range(4)], axis=1)
        out[target, :, 0:lanes] = matmul(flat, own[:, pl.ds(column, lanes)], 1, 0).astype(jnp.bfloat16)
        for block in range(len(parts) // 2):
            total = matmul(near, parts[2 * block][...], 1, 0) + matmul(far, parts[2 * block + 1][...], 1, 0)
            out[target, :, (block + 1) * lanes:(block + 2) * lanes] = total.astype(jnp.bfloat16)


def merge(place, mine, other, own, parts):
    width = parts[0].shape[1] * (1 + len(parts) // 2)
    return pl.pallas_call(
        merge_kernel,
        out_shape=jax.ShapeDtypeStruct((2, mine.shape[1], width), jnp.bfloat16),
        grid_spec=pltpu.PrefetchScalarGridSpec(
            num_scalar_prefetch=1,
            grid=(1,),
            in_specs=[whole(mine.shape), whole(other.shape), whole(own.shape)]
            + [whole(part.shape) for part in parts],
            out_specs=whole((2, mine.shape[1], width)),
        ),
        name="merge",
    )(place, mine, other, own, *parts)


BACK_BY = (0, 1, 3, 2)


def place_kernel(place, got, out):
    cores, cols, _, wide = got.shape
    rows = len(BACK_BY)
    lanes = wide // rows
    for at_core in range(cores):
        for at_col in range(cols):
            for index, back_by in enumerate(BACK_BY):
                at = ((((place[0] + rows - back_by) % rows) * cols + at_col) * cores + at_core) * lanes
                out[:, pl.ds(pl.multiple_of(at, lanes), lanes)] = got[
                    at_core, at_col, :, index * lanes:(index + 1) * lanes]


def place_columns(place, got):
    cores, cols, count, wide = got.shape
    return pl.pallas_call(
        place_kernel,
        out_shape=jax.ShapeDtypeStruct((count, cores * cols * wide), jnp.bfloat16),
        grid_spec=pltpu.PrefetchScalarGridSpec(
            num_scalar_prefetch=1, grid=(1,), in_specs=[whole(got.shape)],
            out_specs=whole((count, cores * cols * wide))),
        name="place_columns",
    )(place, got)


def block_step(tokens, segment_ids, w_qkv, w_out, w_merge, gain_attn, gain_merge):
    rows, cols, planes = lax.axis_size("y"), lax.axis_size("x"), lax.axis_size("z")
    row, col, core = lax.axis_index("y"), lax.axis_index("x"), lax.axis_index("c")
    parity = lax.axis_index("z") % 2
    tok_local = tokens.shape[0]
    groups = tok_local // 4
    row_count = cols * tok_local
    half = D // 2
    wide = w_qkv.shape[1]
    place = jnp.stack([row, core, col, parity]).astype(jnp.int32)
    segments = segment_ids.reshape(rows * cols, groups, 4).transpose(0, 2, 1).reshape(-1)
    layout = attention_inputs(segments, segment_ids)
    row_tokens = lax.all_to_all(
        spread_tokens(tokens, cols), "x", split_axis=0, concat_axis=0, tiled=True)

    weights = w_qkv.T
    own = jnp.concatenate([
        lax.dynamic_slice_in_dim(weights, core * half, half, 1),
        lax.dynamic_slice_in_dim(w_out, core * half, half, 1)], axis=0)
    ahead = [shift_rows(own, step, rows) for step in (3, 2, 1)]
    other_qkv = swap_cores(jnp.stack([part[:wide] for part in ahead]))

    piece = (w_merge.shape[0] // 2, w_merge.shape[1] // 2)
    own_piece = lax.dynamic_slice(w_merge, (parity * piece[0], core * piece[1]), piece)
    first_y = shift_rows(own_piece, 1, rows)
    third_y = shift_rows(own_piece, 3, rows)

    qkv = project_qkv(
        place, row_tokens, gain_attn, weights, ahead, other_qkv, rows)
    by_head = lax.all_to_all(qkv, "y", split_axis=0, concat_axis=0, tiled=True)

    out_rows = jnp.stack([own[wide:]] + [part[wide:] for part in ahead])
    next_out = shift_cols(out_rows, 1, cols)
    out_parts = [out_rows, next_out] + [shift_cols(out_rows, step, cols) for step in (2, 3)]
    first_z = shift_planes(first_y, 1, planes)
    third_z = shift_planes(third_y, planes - 1, planes)
    second_y = shift_rows(own_piece, 2, rows)

    attended = attention(by_head, layout, cols)
    back = lax.all_to_all(
        attended.reshape(rows * cols, HEAD_DIM, row_count), ("y", "x"),
        split_axis=0, concat_axis=0, tiled=True)
    second_z = shift_planes(second_y, 1, planes)
    mine_out = jnp.stack(out_parts)
    other_out = swap_cores(mine_out)
    merged = merge_rows(
        place, back, row_tokens, mine_out, other_out, gain_merge)
    merged = merged.reshape(4, cols * groups, D)
    other_merged = swap_cores(merged)
    block = merge(
        place, merged, other_merged, w_merge, (first_y, first_z, third_y, third_z, second_y, second_z))
    got = lax.all_to_all(
        block.reshape(2 * cols, groups, block.shape[2]), ("c", "x"), split_axis=0, concat_axis=0, tiled=True)
    return place_columns(place, got.reshape(2, cols, groups, block.shape[2]))


def solution(mesh):
    torus = Mesh(mesh.devices.reshape(mesh.shape["dp"] // 2, 2, 4, 4), ("z", "c", "y", "x"))
    dp, seq, both = ("z", "c"), ("y", "x"), ("z", "c", "y", "x")
    in_specs = (P(both, None), P(dp), P(None, seq), P(seq, None), P(None, seq), P(), P())
    return jax.shard_map(block_step, mesh=torus, in_specs=in_specs, out_specs=P(both, None), check_vma=False)
```

```python
import jax
import jax.numpy as jnp
from jax import lax
from jax.experimental import pallas as pl
from jax.experimental.pallas import tpu as pltpu
from jax.sharding import Mesh
from jax.sharding import PartitionSpec as P


D = 1280
HEADS = 16
HEAD_DIM = 80
TQ = 512
TK = 512
LOG2E = 1.4426950408889634


def layer_norm(vector, scale_gain):
    average = jnp.mean(vector, axis=-1, keepdims=True)
    centred = vector - average
    spread_sq = jnp.mean(centred * centred, axis=-1, keepdims=True)
    return centred * lax.rsqrt(spread_sq + 1e-06) * scale_gain


def swap_cores(value):
    return lax.ppermute(value, "c", [(0, 1), (1, 0)])


def shift_rows(value, step, rows):
    return lax.ppermute(value, "y", [(at, (at + step) % rows) for at in range(rows)])


def attention_kernel(bounds, qkv, seg_col, seg_row, out, keys, seg_wide):
    tiles, _, chunk = qkv.shape
    step = pl.program_id(0)
    per_chunk = chunk // TK

    @pl.when(step == 0)
    def _():
        for index in range(tiles):
            keys[index * chunk:(index + 1) * chunk, :] = qkv[index, HEAD_DIM:2 * HEAD_DIM, :].T
        seg_wide[...] = jnp.broadcast_to(seg_col[...], seg_wide.shape)

    part = step // (chunk // TQ)
    offset = pl.multiple_of((step % (chunk // TQ)) * TQ, TQ)
    queries = qkv[part, 0:HEAD_DIM, pl.ds(offset, TQ)]
    query_seg = seg_row[0:1, pl.ds(pl.multiple_of(step * TQ, TQ), TQ)]
    factor = (HEAD_DIM ** -0.5) * LOG2E

    def body(tile, carry):
        top, total, acc = carry
        start = pl.multiple_of(tile * TK, TK)
        scores = lax.dot_general(
            keys[pl.ds(start, TK), :], queries, (((1,), (0,)), ((), ())),
            preferred_element_type=jnp.float32)
        wide = seg_wide[pl.ds(start, TK), :]
        same = jnp.concatenate([wide] * (TQ // 128), axis=1) == query_seg
        scores = jnp.where(same, scores, -jnp.inf)
        new_top = jnp.maximum(top, jnp.max(scores, axis=0, keepdims=True))
        safe = jnp.where(new_top == -jnp.inf, 0.0, new_top)
        decay = jnp.exp2((top - safe) * factor)
        expo = jnp.exp2((scores - safe) * factor)
        total = total * decay + jnp.sum(expo, axis=0, keepdims=True)
        values = qkv[tile // per_chunk, 2 * HEAD_DIM:3 * HEAD_DIM,
                     pl.ds(pl.multiple_of((tile % per_chunk) * TK, TK), TK)]
        acc = acc * decay + lax.dot_general(
            values, expo.astype(jnp.bfloat16), (((1,), (0,)), ((), ())),
            preferred_element_type=jnp.float32)
        return new_top, total, acc

    first, last = bounds[0, step], bounds[1, step]
    _, total, acc = lax.fori_loop(
        first, last, body,
        (jnp.full((1, TQ), -jnp.inf, jnp.float32), jnp.zeros((1, TQ), jnp.float32),
         jnp.zeros((HEAD_DIM, TQ), jnp.float32)))
    result = (acc / total).astype(jnp.bfloat16)
    for copy in range(out.shape[1]):
        out[0, copy] = result


def attention_inputs(segments, segment_ids):
    edges = segment_ids.reshape(-1, TK)
    key_low, key_high = edges[:, 0], edges[:, -1]
    query_edges = segment_ids.reshape(-1, TQ)
    query_low, query_high = query_edges[:, 0], query_edges[:, -1]
    first = jnp.sum(key_high[None, :] < query_low[:, None], axis=1)
    last = jnp.sum(key_low[None, :] <= query_high[:, None], axis=1)
    bounds = jnp.stack([first, last]).astype(jnp.int32)
    return bounds, segments[:, None], segments[None, :]


def attention(qkv, layout, copies):
    tiles, _, chunk = qkv.shape
    count = tiles * chunk
    bounds, seg_col, seg_row = layout
    per = chunk // TQ
    return pl.pallas_call(
        attention_kernel,
        out_shape=jax.ShapeDtypeStruct((tiles, copies, HEAD_DIM, chunk), jnp.bfloat16),
        grid_spec=pltpu.PrefetchScalarGridSpec(
            num_scalar_prefetch=1,
            grid=(count // TQ,),
            in_specs=[
                pl.BlockSpec(qkv.shape, lambda i, b: (0, 0, 0)),
                pl.BlockSpec((count, 1), lambda i, b: (0, 0)),
                pl.BlockSpec((1, count), lambda i, b: (0, 0)),
            ],
            out_specs=pl.BlockSpec((1, copies, HEAD_DIM, TQ), lambda i, b: (i // per, 0, 0, i % per)),
            scratch_shapes=[pltpu.VMEM((count, HEAD_DIM), jnp.bfloat16), pltpu.VMEM((count, 128), jnp.int32)],
        ),
        name="attention",
    )(bounds, qkv, seg_col, seg_row)


def shift_cols(value, step, cols):
    return lax.ppermute(value, "x", [(at, (at + step) % cols) for at in range(cols)])


def shift_planes(value, step, planes):
    return lax.ppermute(value, "z", [(at, (at + step) % planes) for at in range(planes)])


def matmul(left, right, left_dim, right_dim):
    return lax.dot_general(
        left, right, (((left_dim,), (right_dim,)), ((), ())), preferred_element_type=jnp.float32)


def whole(shape):
    return pl.BlockSpec(shape, lambda *_: (0,) * len(shape))


def spread_kernel(tokens, out, wide):
    copies, count, _ = out.shape
    group = count // 4
    for lane in range(wide.shape[0]):
        wide[lane] = tokens[:, lane * 128:(lane + 1) * 128].astype(jnp.float32)
        for spot in range(4):
            part = wide[lane, pl.ds(spot, group, stride=4), :].astype(jnp.bfloat16)
            for copy in range(copies):
                out[copy, spot * group:(spot + 1) * group, lane * 128:(lane + 1) * 128] = part


def spread_tokens(tokens, copies):
    count, width = tokens.shape
    return pl.pallas_call(
        spread_kernel,
        out_shape=jax.ShapeDtypeStruct((copies, count, width), jnp.bfloat16),
        grid=(1,),
        in_specs=[whole(tokens.shape)],
        out_specs=whole((copies, count, width)),
        scratch_shapes=[pltpu.VMEM((width // 128, count, 128), jnp.float32)],
        name="spread",
    )(tokens)


def qkv_kernel(place, tokens, gain, own, first, second, third, other, out, normed):
    row, core = place[0], place[1]
    rows, wide, _ = out.shape
    half = D // 2
    count = normed.shape[0]
    value = layer_norm(tokens[...].reshape(count, D).astype(jnp.float32), gain[...])
    normed[...] = value.astype(jnp.bfloat16)
    out[row] = matmul(own[...], normed[...], 1, 1).astype(jnp.bfloat16)
    mine = normed[:, pl.ds(pl.multiple_of(core * half, half), half)]
    rest = normed[:, pl.ds(pl.multiple_of((1 - core) * half, half), half)]
    for index, part in enumerate((first, second, third)):
        value = matmul(part[0:wide, :], mine, 1, 1) + matmul(other[index], rest, 1, 1)
        out[(row + 1 + index) % rows] = value.astype(jnp.bfloat16)


def project_qkv(place, row_tokens, gain, weights, parts, other, rows):
    cols, count, _ = row_tokens.shape
    wide = weights.shape[0]
    return pl.pallas_call(
        qkv_kernel,
        out_shape=jax.ShapeDtypeStruct((rows, wide, cols * count), jnp.bfloat16),
        grid_spec=pltpu.PrefetchScalarGridSpec(
            num_scalar_prefetch=1,
            grid=(cols // 2,),
            in_specs=[pl.BlockSpec((2, count, D), lambda i, p: (i, 0, 0)), whole((D,)), whole(weights.shape)]
            + [whole(part.shape) for part in parts] + [whole(other.shape)],
            out_specs=pl.BlockSpec((rows, wide, 2 * count), lambda i, p: (0, 0, i)),
            scratch_shapes=[pltpu.VMEM((2 * count, D), jnp.bfloat16)],
        ),
        name="project_qkv",
    )(place, row_tokens, gain, weights, *parts, other)


def hidden_kernel(place, back, residual, mine, other, gain, out, left, hidden):
    row, core, col = place[0], place[1], place[2]
    cols, rows = mine.shape[0], mine.shape[1]
    half = D // 2
    count = hidden.shape[0]
    for at_col in range(cols):
        for at_row in range(rows):
            head = ((row + at_row) % rows) * cols + (col + cols - at_col) % cols
            at = (at_col * rows + at_row) * HEAD_DIM
            left[at:at + HEAD_DIM, :] = back[head]
    turned = left[...].T
    hidden[:, pl.ds(pl.multiple_of(core * half, half), half)] = matmul(turned, mine[...].reshape(D, half), 1, 0)
    hidden[:, pl.ds(pl.multiple_of((1 - core) * half, half), half)] = matmul(
        turned, other[...].reshape(D, half), 1, 0)
    total = residual[...].reshape(count, D).astype(jnp.float32) + hidden[...]
    value = layer_norm(total, gain[...]).astype(jnp.bfloat16)
    group = count // 4
    for spot in range(4):
        out[spot, 0] = value[spot * group:(spot + 1) * group, :]


def merge_rows(place, back, row_tokens, mine, other, gain):
    cols, count, _ = row_tokens.shape
    return pl.pallas_call(
        hidden_kernel,
        out_shape=jax.ShapeDtypeStruct((4, cols, count // 4, D), jnp.bfloat16),
        grid_spec=pltpu.PrefetchScalarGridSpec(
            num_scalar_prefetch=1,
            grid=(cols,),
            in_specs=[
                pl.BlockSpec((HEADS, HEAD_DIM, count), lambda i, p: (0, 0, i)),
                pl.BlockSpec((1, count, D), lambda i, p: (i, 0, 0)),
                whole(mine.shape), whole(other.shape), whole((D,)),
            ],
            out_specs=pl.BlockSpec((4, 1, count // 4, D), lambda i, p: (0, i, 0, 0)),
            scratch_shapes=[pltpu.VMEM((D, count), jnp.bfloat16), pltpu.VMEM((count, D), jnp.float32)],
        ),
        name="merge_rows",
    )(place, back, row_tokens, mine, other, gain)


def merge_kernel(place, mine, other, own, *rest):
    parts, out = rest[:-1], rest[-1]
    core, parity = place[1], place[3]
    lanes = parts[0].shape[1]
    column = pl.multiple_of(core * lanes, lanes)
    for source, target in ((mine, core), (other, 1 - core)):
        near = jnp.concatenate([source[parity * 2], source[parity * 2 + 1]], axis=1)
        far = jnp.concatenate([source[2 - parity * 2], source[3 - parity * 2]], axis=1)
        flat = jnp.concatenate([source[spot] for spot in range(4)], axis=1)
        out[target, :, 0:lanes] = matmul(flat, own[:, pl.ds(column, lanes)], 1, 0).astype(jnp.bfloat16)
        for block in range(3):
            total = 0.0
            for value, pieces in zip((near, far), (parts[block * 2:], parts[block * 2 + 1:])):
                if block < 2:
                    total = total + matmul(value, pieces[0][...], 1, 0)
                else:
                    for index, part in enumerate((pieces[0], pieces[2])):
                        total = total + matmul(value[:, index * D:(index + 1) * D], part[...], 1, 0)
            out[target, :, (block + 1) * lanes:(block + 2) * lanes] = total.astype(jnp.bfloat16)


def merge(place, mine, other, own, parts):
    first_y, first_z, third_y, third_z, second_y, second_z = parts
    parts = first_y + first_z + third_y + third_z + [second_y[0], second_z[0], second_y[1], second_z[1]]
    width = 4 * parts[0].shape[1]
    return pl.pallas_call(
        merge_kernel,
        out_shape=jax.ShapeDtypeStruct((2, mine.shape[1], width), jnp.bfloat16),
        grid_spec=pltpu.PrefetchScalarGridSpec(
            num_scalar_prefetch=1,
            grid=(1,),
            in_specs=[whole(mine.shape), whole(other.shape), whole(own.shape)]
            + [whole(part.shape) for part in parts],
            out_specs=whole((2, mine.shape[1], width)),
        ),
        name="merge",
    )(place, mine, other, own, *parts)


BACK_BY = (0, 1, 3, 2)


def place_kernel(place, got, out):
    cores, cols, _, wide = got.shape
    rows = len(BACK_BY)
    lanes = wide // rows
    for at_core in range(cores):
        for at_col in range(cols):
            for index, back_by in enumerate(BACK_BY):
                at = ((((place[0] + rows - back_by) % rows) * cols + at_col) * cores + at_core) * lanes
                out[:, pl.ds(pl.multiple_of(at, lanes), lanes)] = got[
                    at_core, at_col, :, index * lanes:(index + 1) * lanes]


def place_columns(place, got):
    cores, cols, count, wide = got.shape
    return pl.pallas_call(
        place_kernel,
        out_shape=jax.ShapeDtypeStruct((count, cores * cols * wide), jnp.bfloat16),
        grid_spec=pltpu.PrefetchScalarGridSpec(
            num_scalar_prefetch=1, grid=(1,), in_specs=[whole(got.shape)],
            out_specs=whole((count, cores * cols * wide))),
        name="place_columns",
    )(place, got)


def block_step(tokens, segment_ids, w_qkv, w_out, w_merge, gain_attn, gain_merge):
    rows, cols, planes = lax.axis_size("y"), lax.axis_size("x"), lax.axis_size("z")
    row, col, core = lax.axis_index("y"), lax.axis_index("x"), lax.axis_index("c")
    parity = lax.axis_index("z") % 2
    tok_local = tokens.shape[0]
    groups = tok_local // 4
    row_count = cols * tok_local
    half = D // 2
    wide = w_qkv.shape[1]
    place = jnp.stack([row, core, col, parity]).astype(jnp.int32)
    segments = segment_ids.reshape(rows * cols, groups, 4).transpose(0, 2, 1).reshape(-1)
    layout = attention_inputs(segments, segment_ids)
    row_tokens = lax.all_to_all(
        spread_tokens(tokens, cols), "x", split_axis=0, concat_axis=0, tiled=True)

    weights = w_qkv.T
    own = jnp.concatenate([
        lax.dynamic_slice_in_dim(weights, core * half, half, 1),
        lax.dynamic_slice_in_dim(w_out, core * half, half, 1)], axis=0)
    up, down = shift_rows(own, 1, rows), shift_rows(own, 3, rows)
    cut = own.shape[0] // 2
    across = [shift_rows(up[:cut], 1, rows), shift_rows(down[cut:], 3, rows)]
    ahead = [down, jnp.concatenate(across, axis=0), up]
    other_qkv = swap_cores(jnp.stack([part[:wide] for part in ahead]))

    piece = (w_merge.shape[0] // 2, w_merge.shape[1] // 2)
    own_piece = lax.dynamic_slice(w_merge, (parity * piece[0], core * piece[1]), piece)
    first_y = shift_rows(own_piece, 1, rows)
    third_y = shift_rows(own_piece, 3, rows)

    qkv = project_qkv(
        place, row_tokens, gain_attn, weights, ahead, other_qkv, rows)
    by_head = lax.all_to_all(qkv, "y", split_axis=0, concat_axis=0, tiled=True)

    out_rows = jnp.stack([own[wide:]] + [part[wide:] for part in ahead])
    next_out = shift_cols(out_rows, 1, cols)
    out_parts = [out_rows, next_out] + [shift_cols(out_rows, step, cols) for step in (2, 3)]
    first_z = shift_planes(first_y, 1, planes)
    third_z = shift_planes(third_y, planes - 1, planes)
    cut = piece[0] // 2
    second_y = [shift_rows(first_y[:cut], 1, rows), shift_rows(third_y[cut:], 3, rows)]

    attended = attention(by_head, layout, cols)
    back = lax.all_to_all(
        attended.reshape(rows * cols, HEAD_DIM, row_count), ("y", "x"),
        split_axis=0, concat_axis=0, tiled=True)
    second_z = [shift_planes(second_y[0], 1, planes), shift_planes(second_y[1], planes - 1, planes)]
    mine_out = jnp.stack(out_parts)
    other_out = swap_cores(mine_out)
    merged = merge_rows(
        place, back, row_tokens, mine_out, other_out, gain_merge)
    merged = merged.reshape(4, cols * groups, D)
    other_merged = swap_cores(merged)
    block = merge(
        place, merged, other_merged, w_merge, ([first_y], [first_z], [third_y], [third_z], second_y, second_z))
    got = lax.all_to_all(
        block.reshape(2 * cols, groups, block.shape[2]), ("c", "x"), split_axis=0, concat_axis=0, tiled=True)
    return place_columns(place, got.reshape(2, cols, groups, block.shape[2]))


def solution(mesh):
    torus = Mesh(mesh.devices.reshape(mesh.shape["dp"] // 2, 2, 4, 4), ("z", "c", "y", "x"))
    dp, seq, both = ("z", "c"), ("y", "x"), ("z", "c", "y", "x")
    in_specs = (P(both, None), P(dp), P(None, seq), P(seq, None), P(None, seq), P(), P())
    return jax.shard_map(block_step, mesh=torus, in_specs=in_specs, out_specs=P(both, None), check_vma=False)
```

```python
import jax
import jax.numpy as jnp
from jax import lax
from jax.experimental import pallas as pl
from jax.experimental.pallas import tpu as pltpu
from jax.sharding import Mesh
from jax.sharding import PartitionSpec as P


D = 1280
HEADS = 16
HEAD_DIM = 80
TQ = 512
TK = 512
LOG2E = 1.4426950408889634


def layer_norm(vector, scale_gain):
    average = jnp.mean(vector, axis=-1, keepdims=True)
    centred = vector - average
    spread_sq = jnp.mean(centred * centred, axis=-1, keepdims=True)
    return centred * lax.rsqrt(spread_sq + 1e-06) * scale_gain


def swap_cores(value):
    return lax.ppermute(value, "c", [(0, 1), (1, 0)])


def shift_rows(value, step, rows):
    return lax.ppermute(value, "y", [(at, (at + step) % rows) for at in range(rows)])


def attention_kernel(bounds, qkv, seg_col, seg_row, out, keys, seg_wide):
    tiles, _, chunk = qkv.shape
    step = pl.program_id(0)
    per_chunk = chunk // TK

    @pl.when(step == 0)
    def _():
        for index in range(tiles):
            keys[index * chunk:(index + 1) * chunk, :] = qkv[index, HEAD_DIM:2 * HEAD_DIM, :].T
        seg_wide[...] = jnp.broadcast_to(seg_col[...], seg_wide.shape)

    part = step // (chunk // TQ)
    offset = pl.multiple_of((step % (chunk // TQ)) * TQ, TQ)
    queries = qkv[part, 0:HEAD_DIM, pl.ds(offset, TQ)]
    query_seg = seg_row[0:1, pl.ds(pl.multiple_of(step * TQ, TQ), TQ)]
    factor = (HEAD_DIM ** -0.5) * LOG2E

    def body(tile, carry):
        top, total, acc = carry
        start = pl.multiple_of(tile * TK, TK)
        scores = lax.dot_general(
            keys[pl.ds(start, TK), :], queries, (((1,), (0,)), ((), ())),
            preferred_element_type=jnp.float32)
        wide = seg_wide[pl.ds(start, TK), :]
        same = jnp.concatenate([wide] * (TQ // 128), axis=1) == query_seg
        scores = jnp.where(same, scores, -jnp.inf)
        new_top = jnp.maximum(top, jnp.max(scores, axis=0, keepdims=True))
        safe = jnp.where(new_top == -jnp.inf, 0.0, new_top)
        decay = jnp.exp2((top - safe) * factor)
        expo = jnp.exp2((scores - safe) * factor)
        total = total * decay + jnp.sum(expo, axis=0, keepdims=True)
        values = qkv[tile // per_chunk, 2 * HEAD_DIM:3 * HEAD_DIM,
                     pl.ds(pl.multiple_of((tile % per_chunk) * TK, TK), TK)]
        acc = acc * decay + lax.dot_general(
            values, expo.astype(jnp.bfloat16), (((1,), (0,)), ((), ())),
            preferred_element_type=jnp.float32)
        return new_top, total, acc

    first, last = bounds[0, step], bounds[1, step]
    _, total, acc = lax.fori_loop(
        first, last, body,
        (jnp.full((1, TQ), -jnp.inf, jnp.float32), jnp.zeros((1, TQ), jnp.float32),
         jnp.zeros((HEAD_DIM, TQ), jnp.float32)))
    result = (acc / total).astype(jnp.bfloat16)
    for copy in range(out.shape[1]):
        out[0, copy] = result


def attention_inputs(segments, segment_ids):
    edges = segment_ids.reshape(-1, TK)
    key_low, key_high = edges[:, 0], edges[:, -1]
    query_edges = segment_ids.reshape(-1, TQ)
    query_low, query_high = query_edges[:, 0], query_edges[:, -1]
    first = jnp.sum(key_high[None, :] < query_low[:, None], axis=1)
    last = jnp.sum(key_low[None, :] <= query_high[:, None], axis=1)
    bounds = jnp.stack([first, last]).astype(jnp.int32)
    return bounds, segments[:, None], segments[None, :]


def attention(qkv, layout, copies):
    tiles, _, chunk = qkv.shape
    count = tiles * chunk
    bounds, seg_col, seg_row = layout
    per = chunk // TQ
    return pl.pallas_call(
        attention_kernel,
        out_shape=jax.ShapeDtypeStruct((tiles, copies, HEAD_DIM, chunk), jnp.bfloat16),
        grid_spec=pltpu.PrefetchScalarGridSpec(
            num_scalar_prefetch=1,
            grid=(count // TQ,),
            in_specs=[
                pl.BlockSpec(qkv.shape, lambda i, b: (0, 0, 0)),
                pl.BlockSpec((count, 1), lambda i, b: (0, 0)),
                pl.BlockSpec((1, count), lambda i, b: (0, 0)),
            ],
            out_specs=pl.BlockSpec((1, copies, HEAD_DIM, TQ), lambda i, b: (i // per, 0, 0, i % per)),
            scratch_shapes=[pltpu.VMEM((count, HEAD_DIM), jnp.bfloat16), pltpu.VMEM((count, 128), jnp.int32)],
        ),
        name="attention",
    )(bounds, qkv, seg_col, seg_row)


def shift_cols(value, step, cols):
    return lax.ppermute(value, "x", [(at, (at + step) % cols) for at in range(cols)])


def matmul(left, right, left_dim, right_dim):
    return lax.dot_general(
        left, right, (((left_dim,), (right_dim,)), ((), ())), preferred_element_type=jnp.float32)


def whole(shape):
    return pl.BlockSpec(shape, lambda *_: (0,) * len(shape))


def spread_kernel(tokens, out, wide):
    copies, count, _ = out.shape
    group = count // 4
    for lane in range(wide.shape[0]):
        wide[lane] = tokens[:, lane * 128:(lane + 1) * 128].astype(jnp.float32)
        for spot in range(4):
            part = wide[lane, pl.ds(spot, group, stride=4), :].astype(jnp.bfloat16)
            for copy in range(copies):
                out[copy, spot * group:(spot + 1) * group, lane * 128:(lane + 1) * 128] = part


def spread_tokens(tokens, copies):
    count, width = tokens.shape
    return pl.pallas_call(
        spread_kernel,
        out_shape=jax.ShapeDtypeStruct((copies, count, width), jnp.bfloat16),
        grid=(1,),
        in_specs=[whole(tokens.shape)],
        out_specs=whole((copies, count, width)),
        scratch_shapes=[pltpu.VMEM((width // 128, count, 128), jnp.float32)],
        name="spread",
    )(tokens)


def qkv_kernel(place, tokens, gain, own, first, second, third, other, out, normed):
    row, core = place[0], place[1]
    rows, wide, _ = out.shape
    half = D // 2
    count = normed.shape[0]
    value = layer_norm(tokens[...].reshape(count, D).astype(jnp.float32), gain[...])
    normed[...] = value.astype(jnp.bfloat16)
    out[row] = matmul(own[...], normed[...], 1, 1).astype(jnp.bfloat16)
    mine = normed[:, pl.ds(pl.multiple_of(core * half, half), half)]
    rest = normed[:, pl.ds(pl.multiple_of((1 - core) * half, half), half)]
    for index, part in enumerate((first, second, third)):
        value = matmul(part[0:wide, :], mine, 1, 1) + matmul(other[index], rest, 1, 1)
        out[(row + 1 + index) % rows] = value.astype(jnp.bfloat16)


def project_qkv(place, row_tokens, gain, weights, parts, other, rows):
    cols, count, _ = row_tokens.shape
    wide = weights.shape[0]
    return pl.pallas_call(
        qkv_kernel,
        out_shape=jax.ShapeDtypeStruct((rows, wide, cols * count), jnp.bfloat16),
        grid_spec=pltpu.PrefetchScalarGridSpec(
            num_scalar_prefetch=1,
            grid=(cols // 2,),
            in_specs=[pl.BlockSpec((2, count, D), lambda i, p: (i, 0, 0)), whole((D,)), whole(weights.shape)]
            + [whole(part.shape) for part in parts] + [whole(other.shape)],
            out_specs=pl.BlockSpec((rows, wide, 2 * count), lambda i, p: (0, 0, i)),
            scratch_shapes=[pltpu.VMEM((2 * count, D), jnp.bfloat16)],
        ),
        name="project_qkv",
    )(place, row_tokens, gain, weights, *parts, other)


def hidden_kernel(place, back, residual, mine, other, gain, out, left, hidden):
    row, core, col = place[0], place[1], place[2]
    cols, rows = mine.shape[0], mine.shape[1]
    half = D // 2
    count = hidden.shape[0]
    for at_col in range(cols):
        for at_row in range(rows):
            head = ((row + at_row) % rows) * cols + (col + cols - at_col) % cols
            at = (at_col * rows + at_row) * HEAD_DIM
            left[at:at + HEAD_DIM, :] = back[head]
    turned = left[...].T
    hidden[:, pl.ds(pl.multiple_of(core * half, half), half)] = matmul(turned, mine[...].reshape(D, half), 1, 0)
    hidden[:, pl.ds(pl.multiple_of((1 - core) * half, half), half)] = matmul(
        turned, other[...].reshape(D, half), 1, 0)
    total = residual[...].reshape(count, D).astype(jnp.float32) + hidden[...]
    value = layer_norm(total, gain[...]).astype(jnp.bfloat16)
    group = count // 4
    for spot in range(4):
        out[spot, 0] = value[spot * group:(spot + 1) * group, :]


def merge_rows(place, back, row_tokens, mine, other, gain):
    cols, count, _ = row_tokens.shape
    return pl.pallas_call(
        hidden_kernel,
        out_shape=jax.ShapeDtypeStruct((4, cols, count // 4, D), jnp.bfloat16),
        grid_spec=pltpu.PrefetchScalarGridSpec(
            num_scalar_prefetch=1,
            grid=(cols,),
            in_specs=[
                pl.BlockSpec((HEADS, HEAD_DIM, count), lambda i, p: (0, 0, i)),
                pl.BlockSpec((1, count, D), lambda i, p: (i, 0, 0)),
                whole(mine.shape), whole(other.shape), whole((D,)),
            ],
            out_specs=pl.BlockSpec((4, 1, count // 4, D), lambda i, p: (0, i, 0, 0)),
            scratch_shapes=[pltpu.VMEM((D, count), jnp.bfloat16), pltpu.VMEM((count, D), jnp.float32)],
        ),
        name="merge_rows",
    )(place, back, row_tokens, mine, other, gain)


def merge_kernel(place, mine, other, weights, out, flat):
    core = place[1]
    count = mine.shape[1]

    @pl.when(pl.program_id(0) == 0)
    def _():
        for spot in range(4):
            flat[0:count, spot * D:(spot + 1) * D] = mine[spot]
            flat[count:2 * count, spot * D:(spot + 1) * D] = other[spot]

    wide = jnp.concatenate([weights[0], weights[1]], axis=1)
    value = matmul(flat[...], wide, 1, 0).astype(jnp.bfloat16)
    out[core] = value[0:count, :]
    out[1 - core] = value[count:2 * count, :]


def merge(place, mine, other, weights):
    blocks, depth, lanes = weights.shape
    count = mine.shape[1]
    return pl.pallas_call(
        merge_kernel,
        out_shape=jax.ShapeDtypeStruct((2, count, blocks * lanes), jnp.bfloat16),
        grid_spec=pltpu.PrefetchScalarGridSpec(
            num_scalar_prefetch=1,
            grid=(blocks // 2,),
            in_specs=[whole(mine.shape), whole(other.shape),
                      pl.BlockSpec((2, depth, lanes), lambda i, p: (i, 0, 0))],
            out_specs=pl.BlockSpec((2, count, 2 * lanes), lambda i, p: (0, 0, i)),
            scratch_shapes=[pltpu.VMEM((2 * count, depth), jnp.bfloat16)],
        ),
        name="merge",
    )(place, mine, other, weights)


def place_kernel(got, out):
    cores, cols, _, wide = got.shape
    rows = out.shape[1] // (cores * cols * 128)
    lanes = wide // rows
    for at_core in range(cores):
        for at_col in range(cols):
            for at_row in range(rows):
                at = ((at_row * cols + at_col) * cores + at_core) * lanes
                out[:, at:at + lanes] = got[at_core, at_col, :, at_row * lanes:(at_row + 1) * lanes]


def place_columns(got):
    cores, cols, count, wide = got.shape
    return pl.pallas_call(
        place_kernel,
        out_shape=jax.ShapeDtypeStruct((count, cores * cols * wide), jnp.bfloat16),
        grid=(1,), in_specs=[whole(got.shape)],
        out_specs=whole((count, cores * cols * wide)),
        name="place_columns",
    )(got)


def block_step(tokens, segment_ids, w_qkv, w_out, w_merge, gain_attn, gain_merge):
    rows, cols = lax.axis_size("y"), lax.axis_size("x")
    row, col, core = lax.axis_index("y"), lax.axis_index("x"), lax.axis_index("c")
    tok_local = tokens.shape[0]
    groups = tok_local // 4
    row_count = cols * tok_local
    half = D // 2
    wide = w_qkv.shape[1]
    lanes = w_merge.shape[1] // 2
    all_merge = lax.all_gather(lax.dynamic_slice_in_dim(w_merge, core * lanes, lanes, 1), "y", axis=0)
    place = jnp.stack([row, core, col]).astype(jnp.int32)
    segments = segment_ids.reshape(rows * cols, groups, 4).transpose(0, 2, 1).reshape(-1)
    layout = attention_inputs(segments, segment_ids)
    row_tokens = lax.all_to_all(
        spread_tokens(tokens, cols), "x", split_axis=0, concat_axis=0, tiled=True)

    weights = w_qkv.T
    own = jnp.concatenate([
        lax.dynamic_slice_in_dim(weights, core * half, half, 1),
        lax.dynamic_slice_in_dim(w_out, core * half, half, 1)], axis=0)
    ahead = [shift_rows(own, step, rows) for step in (3, 2, 1)]
    other_qkv = swap_cores(jnp.stack([part[:wide] for part in ahead]))

    qkv = project_qkv(
        place, row_tokens, gain_attn, weights, ahead, other_qkv, rows)
    by_head = lax.all_to_all(qkv, "y", split_axis=0, concat_axis=0, tiled=True)

    out_rows = jnp.stack([own[wide:]] + [part[wide:] for part in ahead])
    next_out = shift_cols(out_rows, 1, cols)
    out_parts = [out_rows, next_out] + [shift_cols(out_rows, step, cols) for step in (2, 3)]
    attended = attention(by_head, layout, cols)
    back = lax.all_to_all(
        attended.reshape(rows * cols, HEAD_DIM, row_count), ("y", "x"),
        split_axis=0, concat_axis=0, tiled=True)
    mine_out = jnp.stack(out_parts)
    other_out = swap_cores(mine_out)
    merged = merge_rows(
        place, back, row_tokens, mine_out, other_out, gain_merge)
    merged = merged.reshape(4, cols * groups, D)
    other_merged = swap_cores(merged)
    block = merge(place, merged, other_merged, all_merge)
    got = lax.all_to_all(
        block.reshape(2 * cols, groups, block.shape[2]), ("c", "x"), split_axis=0, concat_axis=0, tiled=True)
    return place_columns(got.reshape(2, cols, groups, block.shape[2]))


def solution(mesh):
    torus = Mesh(mesh.devices.reshape(mesh.shape["dp"] // 2, 2, 4, 4), ("z", "c", "y", "x"))
    dp, seq, both = ("z", "c"), ("y", "x"), ("z", "c", "y", "x")
    in_specs = (P(both, None), P(dp), P(None, seq), P(seq, None), P(None, seq), P(), P())
    return jax.shard_map(block_step, mesh=torus, in_specs=in_specs, out_specs=P(both, None), check_vma=False)
```

```python
import jax
import jax.numpy as jnp
from jax import lax
from jax.experimental import pallas as pl
from jax.experimental.pallas import tpu as pltpu
from jax.sharding import Mesh
from jax.sharding import PartitionSpec as P


D = 1280
HEADS = 16
HEAD_DIM = 80
TQ = 512
TK = 512
LOG2E = 1.4426950408889634


def layer_norm(vector, scale_gain):
    average = jnp.mean(vector, axis=-1, keepdims=True)
    centred = vector - average
    spread_sq = jnp.mean(centred * centred, axis=-1, keepdims=True)
    return centred * lax.rsqrt(spread_sq + 1e-06) * scale_gain


def swap_cores(value):
    return lax.ppermute(value, "c", [(0, 1), (1, 0)])


def shift_rows(value, step, rows):
    return lax.ppermute(value, "y", [(at, (at + step) % rows) for at in range(rows)])


def attention_kernel(bounds, qkv, seg_col, seg_row, out, keys, seg_wide):
    tiles, _, chunk = qkv.shape
    step = pl.program_id(0)
    per_chunk = chunk // TK

    @pl.when(step == 0)
    def _():
        for index in range(tiles):
            keys[index * chunk:(index + 1) * chunk, :] = qkv[index, HEAD_DIM:2 * HEAD_DIM, :].T
        seg_wide[...] = jnp.broadcast_to(seg_col[...], seg_wide.shape)

    part = step // (chunk // TQ)
    offset = pl.multiple_of((step % (chunk // TQ)) * TQ, TQ)
    queries = qkv[part, 0:HEAD_DIM, pl.ds(offset, TQ)]
    query_seg = seg_row[0:1, pl.ds(pl.multiple_of(step * TQ, TQ), TQ)]
    factor = (HEAD_DIM ** -0.5) * LOG2E

    def body(tile, carry):
        top, total, acc = carry
        start = pl.multiple_of(tile * TK, TK)
        scores = lax.dot_general(
            keys[pl.ds(start, TK), :], queries, (((1,), (0,)), ((), ())),
            preferred_element_type=jnp.float32)
        wide = seg_wide[pl.ds(start, TK), :]
        same = jnp.concatenate([wide] * (TQ // 128), axis=1) == query_seg
        scores = jnp.where(same, scores, -jnp.inf)
        new_top = jnp.maximum(top, jnp.max(scores, axis=0, keepdims=True))
        safe = jnp.where(new_top == -jnp.inf, 0.0, new_top)
        decay = jnp.exp2((top - safe) * factor)
        expo = jnp.exp2((scores - safe) * factor)
        total = total * decay + jnp.sum(expo, axis=0, keepdims=True)
        values = qkv[tile // per_chunk, 2 * HEAD_DIM:3 * HEAD_DIM,
                     pl.ds(pl.multiple_of((tile % per_chunk) * TK, TK), TK)]
        acc = acc * decay + lax.dot_general(
            values, expo.astype(jnp.bfloat16), (((1,), (0,)), ((), ())),
            preferred_element_type=jnp.float32)
        return new_top, total, acc

    first, last = bounds[0, step], bounds[1, step]
    _, total, acc = lax.fori_loop(
        first, last, body,
        (jnp.full((1, TQ), -jnp.inf, jnp.float32), jnp.zeros((1, TQ), jnp.float32),
         jnp.zeros((HEAD_DIM, TQ), jnp.float32)))
    result = (acc / total).astype(jnp.bfloat16)
    for copy in range(out.shape[1]):
        out[0, copy] = result


def attention_inputs(segments, segment_ids):
    edges = segment_ids.reshape(-1, TK)
    key_low, key_high = edges[:, 0], edges[:, -1]
    query_edges = segment_ids.reshape(-1, TQ)
    query_low, query_high = query_edges[:, 0], query_edges[:, -1]
    first = jnp.sum(key_high[None, :] < query_low[:, None], axis=1)
    last = jnp.sum(key_low[None, :] <= query_high[:, None], axis=1)
    bounds = jnp.stack([first, last]).astype(jnp.int32)
    return bounds, segments[:, None], segments[None, :]


def attention(qkv, layout, copies):
    tiles, _, chunk = qkv.shape
    count = tiles * chunk
    bounds, seg_col, seg_row = layout
    per = chunk // TQ
    return pl.pallas_call(
        attention_kernel,
        out_shape=jax.ShapeDtypeStruct((tiles, copies, HEAD_DIM, chunk), jnp.bfloat16),
        grid_spec=pltpu.PrefetchScalarGridSpec(
            num_scalar_prefetch=1,
            grid=(count // TQ,),
            in_specs=[
                pl.BlockSpec(qkv.shape, lambda i, b: (0, 0, 0)),
                pl.BlockSpec((count, 1), lambda i, b: (0, 0)),
                pl.BlockSpec((1, count), lambda i, b: (0, 0)),
            ],
            out_specs=pl.BlockSpec((1, copies, HEAD_DIM, TQ), lambda i, b: (i // per, 0, 0, i % per)),
            scratch_shapes=[pltpu.VMEM((count, HEAD_DIM), jnp.bfloat16), pltpu.VMEM((count, 128), jnp.int32)],
        ),
        name="attention",
    )(bounds, qkv, seg_col, seg_row)


def shift_cols(value, step, cols):
    return lax.ppermute(value, "x", [(at, (at + step) % cols) for at in range(cols)])


def shift_planes(value, step, planes):
    return lax.ppermute(value, "z", [(at, (at + step) % planes) for at in range(planes)])


def matmul(left, right, left_dim, right_dim):
    return lax.dot_general(
        left, right, (((left_dim,), (right_dim,)), ((), ())), preferred_element_type=jnp.float32)


def whole(shape):
    return pl.BlockSpec(shape, lambda *_: (0,) * len(shape))


def spread_kernel(tokens, out, wide):
    copies, count, _ = out.shape
    group = count // 4
    for lane in range(wide.shape[0]):
        wide[lane] = tokens[:, lane * 128:(lane + 1) * 128].astype(jnp.float32)
        for spot in range(4):
            part = wide[lane, pl.ds(spot, group, stride=4), :].astype(jnp.bfloat16)
            for copy in range(copies):
                out[copy, spot * group:(spot + 1) * group, lane * 128:(lane + 1) * 128] = part


def spread_tokens(tokens, copies):
    count, width = tokens.shape
    return pl.pallas_call(
        spread_kernel,
        out_shape=jax.ShapeDtypeStruct((copies, count, width), jnp.bfloat16),
        grid=(1,),
        in_specs=[whole(tokens.shape)],
        out_specs=whole((copies, count, width)),
        scratch_shapes=[pltpu.VMEM((width // 128, count, 128), jnp.float32)],
        name="spread",
    )(tokens)


def qkv_kernel(place, tokens, gain, own, first, second, third, other, out, normed):
    row, core = place[0], place[1]
    rows, wide, _ = out.shape
    half = D // 2
    count = normed.shape[0]
    value = layer_norm(tokens[...].reshape(count, D).astype(jnp.float32), gain[...])
    normed[...] = value.astype(jnp.bfloat16)
    out[row] = matmul(own[...], normed[...], 1, 1).astype(jnp.bfloat16)
    mine = normed[:, pl.ds(pl.multiple_of(core * half, half), half)]
    rest = normed[:, pl.ds(pl.multiple_of((1 - core) * half, half), half)]
    for index, part in enumerate((first, second, third)):
        value = matmul(part[0:wide, :], mine, 1, 1) + matmul(other[index], rest, 1, 1)
        out[(row + 1 + index) % rows] = value.astype(jnp.bfloat16)


def project_qkv(place, row_tokens, gain, weights, parts, other, rows):
    cols, count, _ = row_tokens.shape
    wide = weights.shape[0]
    return pl.pallas_call(
        qkv_kernel,
        out_shape=jax.ShapeDtypeStruct((rows, wide, cols * count), jnp.bfloat16),
        grid_spec=pltpu.PrefetchScalarGridSpec(
            num_scalar_prefetch=1,
            grid=(cols // 2,),
            in_specs=[pl.BlockSpec((2, count, D), lambda i, p: (i, 0, 0)), whole((D,)), whole(weights.shape)]
            + [whole(part.shape) for part in parts] + [whole(other.shape)],
            out_specs=pl.BlockSpec((rows, wide, 2 * count), lambda i, p: (0, 0, i)),
            scratch_shapes=[pltpu.VMEM((2 * count, D), jnp.bfloat16)],
        ),
        name="project_qkv",
    )(place, row_tokens, gain, weights, *parts, other)


def hidden_kernel(place, back, residual, mine, other, gain, out, left, hidden):
    row, core, col = place[0], place[1], place[2]
    cols, rows = mine.shape[0], mine.shape[1]
    half = D // 2
    count = hidden.shape[0]
    for at_col in range(cols):
        for at_row in range(rows):
            head = ((row + at_row) % rows) * cols + (col + cols - at_col) % cols
            at = (at_col * rows + at_row) * HEAD_DIM
            left[at:at + HEAD_DIM, :] = back[head]
    turned = left[...].T
    hidden[:, pl.ds(pl.multiple_of(core * half, half), half)] = matmul(turned, mine[...].reshape(D, half), 1, 0)
    hidden[:, pl.ds(pl.multiple_of((1 - core) * half, half), half)] = matmul(
        turned, other[...].reshape(D, half), 1, 0)
    total = residual[...].reshape(count, D).astype(jnp.float32) + hidden[...]
    value = layer_norm(total, gain[...]).astype(jnp.bfloat16)
    group = out.shape[2]
    for index in range(out.shape[1]):
        for spot in range(4):
            at = (index * 4 + spot) * group
            out[spot, index] = value[at:at + group, :]


def merge_rows(place, back, row_tokens, mine, other, gain):
    cols, count, _ = row_tokens.shape
    return pl.pallas_call(
        hidden_kernel,
        out_shape=jax.ShapeDtypeStruct((4, cols, count // 4, D), jnp.bfloat16),
        grid_spec=pltpu.PrefetchScalarGridSpec(
            num_scalar_prefetch=1,
            grid=(cols // 2,),
            in_specs=[
                pl.BlockSpec((HEADS, HEAD_DIM, 2 * count), lambda i, p: (0, 0, i)),
                pl.BlockSpec((2, count, D), lambda i, p: (i, 0, 0)),
                whole(mine.shape), whole(other.shape), whole((D,)),
            ],
            out_specs=pl.BlockSpec((4, 2, count // 4, D), lambda i, p: (0, i, 0, 0)),
            scratch_shapes=[pltpu.VMEM((D, 2 * count), jnp.bfloat16), pltpu.VMEM((2 * count, D), jnp.float32)],
        ),
        name="merge_rows",
    )(place, back, row_tokens, mine, other, gain)


def merge_kernel(place, mine, other, own, *rest):
    parts, out, near, far = rest[:-3], rest[-3], rest[-2], rest[-1]
    core, parity = place[1], place[3]
    lanes = parts[0].shape[1]
    count, depth = mine.shape[1], 2 * D
    for index, source in enumerate((mine, other)):
        for spot in range(2):
            at = (slice(index * count, (index + 1) * count), slice(spot * D, (spot + 1) * D))
            near[at] = source[parity * 2 + spot]
            far[at] = source[2 - parity * 2 + spot]
    column = pl.ds(pl.multiple_of(core * lanes, lanes), lanes)
    near_own = own[pl.ds(pl.multiple_of(parity * depth, depth), depth), column]
    far_own = own[pl.ds(pl.multiple_of((1 - parity) * depth, depth), depth), column]
    near_wide = jnp.concatenate([near_own] + [part[...] for part in parts[0::2]], axis=1)
    far_wide = jnp.concatenate([far_own] + [part[...] for part in parts[1::2]], axis=1)
    value = matmul(near[...], near_wide, 1, 0) + matmul(far[...], far_wide, 1, 0)
    out[core] = value[0:count, :].astype(jnp.bfloat16)
    out[1 - core] = value[count:2 * count, :].astype(jnp.bfloat16)


def merge(place, mine, other, own, parts):
    width = parts[0].shape[1] * (1 + len(parts) // 2)
    return pl.pallas_call(
        merge_kernel,
        out_shape=jax.ShapeDtypeStruct((2, mine.shape[1], width), jnp.bfloat16),
        grid_spec=pltpu.PrefetchScalarGridSpec(
            num_scalar_prefetch=1,
            grid=(1,),
            in_specs=[whole(mine.shape), whole(other.shape), whole(own.shape)]
            + [whole(part.shape) for part in parts],
            out_specs=whole((2, mine.shape[1], width)),
            scratch_shapes=[pltpu.VMEM((2 * mine.shape[1], 2 * D), jnp.bfloat16)] * 2,
        ),
        name="merge",
    )(place, mine, other, own, *parts)


BACK_BY = (0, 1, 3, 2)


def place_kernel(place, got, out):
    cores, cols, _, wide = got.shape
    rows = len(BACK_BY)
    lanes = wide // rows
    for at_core in range(cores):
        for at_col in range(cols):
            for index, back_by in enumerate(BACK_BY):
                at = ((((place[0] + rows - back_by) % rows) * cols + at_col) * cores + at_core) * lanes
                out[:, pl.ds(pl.multiple_of(at, lanes), lanes)] = got[
                    at_core, at_col, :, index * lanes:(index + 1) * lanes]


def place_columns(place, got):
    cores, cols, count, wide = got.shape
    return pl.pallas_call(
        place_kernel,
        out_shape=jax.ShapeDtypeStruct((count, cores * cols * wide), jnp.bfloat16),
        grid_spec=pltpu.PrefetchScalarGridSpec(
            num_scalar_prefetch=1, grid=(1,), in_specs=[whole(got.shape)],
            out_specs=whole((count, cores * cols * wide))),
        name="place_columns",
    )(place, got)


def block_step(tokens, segment_ids, w_qkv, w_out, w_merge, gain_attn, gain_merge):
    rows, cols, planes = lax.axis_size("y"), lax.axis_size("x"), lax.axis_size("z")
    row, col, core = lax.axis_index("y"), lax.axis_index("x"), lax.axis_index("c")
    parity = lax.axis_index("z") % 2
    tok_local = tokens.shape[0]
    groups = tok_local // 4
    row_count = cols * tok_local
    half = D // 2
    wide = w_qkv.shape[1]
    place = jnp.stack([row, core, col, parity]).astype(jnp.int32)
    segments = segment_ids.reshape(rows * cols, groups, 4).transpose(0, 2, 1).reshape(-1)
    layout = attention_inputs(segments, segment_ids)
    row_tokens = lax.all_to_all(
        spread_tokens(tokens, cols), "x", split_axis=0, concat_axis=0, tiled=True)

    weights = w_qkv.T
    own = jnp.concatenate([
        lax.dynamic_slice_in_dim(weights, core * half, half, 1),
        lax.dynamic_slice_in_dim(w_out, core * half, half, 1)], axis=0)
    ahead = [shift_rows(own, step, rows) for step in (3, 2, 1)]
    other_qkv = swap_cores(jnp.stack([part[:wide] for part in ahead]))

    piece = (w_merge.shape[0] // 2, w_merge.shape[1] // 2)
    own_piece = lax.dynamic_slice(w_merge, (parity * piece[0], core * piece[1]), piece)
    first_y = shift_rows(own_piece, 1, rows)
    third_y = shift_rows(own_piece, 3, rows)

    qkv = project_qkv(
        place, row_tokens, gain_attn, weights, ahead, other_qkv, rows)
    by_head = lax.all_to_all(qkv, "y", split_axis=0, concat_axis=0, tiled=True)

    out_rows = jnp.stack([own[wide:]] + [part[wide:] for part in ahead])
    next_out = shift_cols(out_rows, 1, cols)
    out_parts = [out_rows, next_out] + [shift_cols(out_rows, step, cols) for step in (2, 3)]
    first_z = shift_planes(first_y, 1, planes)
    third_z = shift_planes(third_y, planes - 1, planes)
    second_y = shift_rows(first_y, 1, rows)

    attended = attention(by_head, layout, cols)
    back = lax.all_to_all(
        attended.reshape(rows * cols, HEAD_DIM, row_count), ("y", "x"),
        split_axis=0, concat_axis=0, tiled=True)
    second_z = shift_planes(second_y, 1, planes)
    mine_out = jnp.stack(out_parts)
    other_out = swap_cores(mine_out)
    merged = merge_rows(
        place, back, row_tokens, mine_out, other_out, gain_merge)
    merged = merged.reshape(4, cols * groups, D)
    other_merged = swap_cores(merged)
    block = merge(
        place, merged, other_merged, w_merge, (first_y, first_z, third_y, third_z, second_y, second_z))
    got = lax.all_to_all(
        block.reshape(2 * cols, groups, block.shape[2]), ("c", "x"), split_axis=0, concat_axis=0, tiled=True)
    return place_columns(place, got.reshape(2, cols, groups, block.shape[2]))


def solution(mesh):
    torus = Mesh(mesh.devices.reshape(mesh.shape["dp"] // 2, 2, 4, 4), ("z", "c", "y", "x"))
    dp, seq, both = ("z", "c"), ("y", "x"), ("z", "c", "y", "x")
    in_specs = (P(both, None), P(dp), P(None, seq), P(seq, None), P(None, seq), P(), P())
    return jax.shard_map(block_step, mesh=torus, in_specs=in_specs, out_specs=P(both, None), check_vma=False)
```

```python
import jax
import jax.numpy as jnp
from jax import lax
from jax.experimental import pallas as pl
from jax.experimental.pallas import tpu as pltpu
from jax.sharding import Mesh
from jax.sharding import PartitionSpec as P


D = 1280
HEADS = 16
HEAD_DIM = 80
TQ = 512
TK = 512
LOG2E = 1.4426950408889634


def layer_norm(vector, scale_gain):
    average = jnp.mean(vector, axis=-1, keepdims=True)
    centred = vector - average
    spread_sq = jnp.mean(centred * centred, axis=-1, keepdims=True)
    return centred * lax.rsqrt(spread_sq + 1e-06) * scale_gain


def swap_cores(value):
    return lax.ppermute(value, "c", [(0, 1), (1, 0)])


def shift_rows(value, step, rows):
    return lax.ppermute(value, "y", [(at, (at + step) % rows) for at in range(rows)])


def attention_kernel(bounds, qkv, seg_col, seg_row, out, keys, seg_wide):
    tiles, _, chunk = qkv.shape
    step = pl.program_id(0)
    per_chunk = chunk // TK

    @pl.when(step == 0)
    def _():
        for index in range(tiles):
            keys[index * chunk:(index + 1) * chunk, :] = qkv[index, HEAD_DIM:2 * HEAD_DIM, :].T
        seg_wide[...] = jnp.broadcast_to(seg_col[...], seg_wide.shape)

    part = step // (chunk // TQ)
    offset = pl.multiple_of((step % (chunk // TQ)) * TQ, TQ)
    queries = qkv[part, 0:HEAD_DIM, pl.ds(offset, TQ)]
    query_seg = seg_row[0:1, pl.ds(pl.multiple_of(step * TQ, TQ), TQ)]
    factor = (HEAD_DIM ** -0.5) * LOG2E

    def body(tile, carry):
        top, total, acc = carry
        start = pl.multiple_of(tile * TK, TK)
        scores = lax.dot_general(
            keys[pl.ds(start, TK), :], queries, (((1,), (0,)), ((), ())),
            preferred_element_type=jnp.float32)
        wide = seg_wide[pl.ds(start, TK), :]
        same = jnp.concatenate([wide] * (TQ // 128), axis=1) == query_seg
        scores = jnp.where(same, scores, -jnp.inf)
        new_top = jnp.maximum(top, jnp.max(scores, axis=0, keepdims=True))
        safe = jnp.where(new_top == -jnp.inf, 0.0, new_top)
        decay = jnp.exp2((top - safe) * factor)
        expo = jnp.exp2((scores - safe) * factor)
        total = total * decay + jnp.sum(expo, axis=0, keepdims=True)
        values = qkv[tile // per_chunk, 2 * HEAD_DIM:3 * HEAD_DIM,
                     pl.ds(pl.multiple_of((tile % per_chunk) * TK, TK), TK)]
        acc = acc * decay + lax.dot_general(
            values, expo.astype(jnp.bfloat16), (((1,), (0,)), ((), ())),
            preferred_element_type=jnp.float32)
        return new_top, total, acc

    first, last = bounds[0, step], bounds[1, step]
    _, total, acc = lax.fori_loop(
        first, last, body,
        (jnp.full((1, TQ), -jnp.inf, jnp.float32), jnp.zeros((1, TQ), jnp.float32),
         jnp.zeros((HEAD_DIM, TQ), jnp.float32)))
    result = (acc / total).astype(jnp.bfloat16)
    for copy in range(out.shape[1]):
        out[0, copy] = result


def attention_inputs(segments, segment_ids):
    edges = segment_ids.reshape(-1, TK)
    key_low, key_high = edges[:, 0], edges[:, -1]
    query_edges = segment_ids.reshape(-1, TQ)
    query_low, query_high = query_edges[:, 0], query_edges[:, -1]
    first = jnp.sum(key_high[None, :] < query_low[:, None], axis=1)
    last = jnp.sum(key_low[None, :] <= query_high[:, None], axis=1)
    bounds = jnp.stack([first, last]).astype(jnp.int32)
    return bounds, segments[:, None], segments[None, :]


def attention(qkv, layout, copies):
    tiles, _, chunk = qkv.shape
    count = tiles * chunk
    bounds, seg_col, seg_row = layout
    per = chunk // TQ
    return pl.pallas_call(
        attention_kernel,
        out_shape=jax.ShapeDtypeStruct((tiles, copies, HEAD_DIM, chunk), jnp.bfloat16),
        grid_spec=pltpu.PrefetchScalarGridSpec(
            num_scalar_prefetch=1,
            grid=(count // TQ,),
            in_specs=[
                pl.BlockSpec(qkv.shape, lambda i, b: (0, 0, 0)),
                pl.BlockSpec((count, 1), lambda i, b: (0, 0)),
                pl.BlockSpec((1, count), lambda i, b: (0, 0)),
            ],
            out_specs=pl.BlockSpec((1, copies, HEAD_DIM, TQ), lambda i, b: (i // per, 0, 0, i % per)),
            scratch_shapes=[pltpu.VMEM((count, HEAD_DIM), jnp.bfloat16), pltpu.VMEM((count, 128), jnp.int32)],
        ),
        name="attention",
    )(bounds, qkv, seg_col, seg_row)


def shift_cols(value, step, cols):
    return lax.ppermute(value, "x", [(at, (at + step) % cols) for at in range(cols)])


def swap_planes(value, planes):
    return lax.ppermute(value, "z", [(at, at ^ 1) for at in range(planes)])


def matmul(left, right, left_dim, right_dim):
    return lax.dot_general(
        left, right, (((left_dim,), (right_dim,)), ((), ())), preferred_element_type=jnp.float32)


def whole(shape):
    return pl.BlockSpec(shape, lambda *_: (0,) * len(shape))


def spread_kernel(tokens, out, wide):
    copies, count, _ = out.shape
    group = count // 4
    for lane in range(wide.shape[0]):
        wide[lane] = tokens[:, lane * 128:(lane + 1) * 128].astype(jnp.float32)
        for spot in range(4):
            part = wide[lane, pl.ds(spot, group, stride=4), :].astype(jnp.bfloat16)
            for copy in range(copies):
                out[copy, spot * group:(spot + 1) * group, lane * 128:(lane + 1) * 128] = part


def spread_tokens(tokens, copies):
    count, width = tokens.shape
    return pl.pallas_call(
        spread_kernel,
        out_shape=jax.ShapeDtypeStruct((copies, count, width), jnp.bfloat16),
        grid=(1,),
        in_specs=[whole(tokens.shape)],
        out_specs=whole((copies, count, width)),
        scratch_shapes=[pltpu.VMEM((width // 128, count, 128), jnp.float32)],
        name="spread",
    )(tokens)


def qkv_kernel(place, tokens, gain, own, first, second, third, other, out, normed):
    row, core = place[0], place[1]
    rows, wide, _ = out.shape
    half = D // 2
    count = normed.shape[0]
    value = layer_norm(tokens[...].reshape(count, D).astype(jnp.float32), gain[...])
    normed[...] = value.astype(jnp.bfloat16)
    out[row] = matmul(own[...], normed[...], 1, 1).astype(jnp.bfloat16)
    mine = normed[:, pl.ds(pl.multiple_of(core * half, half), half)]
    rest = normed[:, pl.ds(pl.multiple_of((1 - core) * half, half), half)]
    for index, part in enumerate((first, second, third)):
        value = matmul(part[0:wide, :], mine, 1, 1) + matmul(other[index], rest, 1, 1)
        out[(row + 1 + index) % rows] = value.astype(jnp.bfloat16)


def project_qkv(place, row_tokens, gain, weights, parts, other, rows):
    cols, count, _ = row_tokens.shape
    wide = weights.shape[0]
    return pl.pallas_call(
        qkv_kernel,
        out_shape=jax.ShapeDtypeStruct((rows, wide, cols * count), jnp.bfloat16),
        grid_spec=pltpu.PrefetchScalarGridSpec(
            num_scalar_prefetch=1,
            grid=(cols // 2,),
            in_specs=[pl.BlockSpec((2, count, D), lambda i, p: (i, 0, 0)), whole((D,)), whole(weights.shape)]
            + [whole(part.shape) for part in parts] + [whole(other.shape)],
            out_specs=pl.BlockSpec((rows, wide, 2 * count), lambda i, p: (0, 0, i)),
            scratch_shapes=[pltpu.VMEM((2 * count, D), jnp.bfloat16)],
        ),
        name="project_qkv",
    )(place, row_tokens, gain, weights, *parts, other)


def hidden_kernel(place, back, residual, mine, other, gain, out, left, hidden):
    row, core, col = place[0], place[1], place[2]
    cols, rows = mine.shape[0], mine.shape[1]
    half = D // 2
    count = hidden.shape[0]
    for at_col in range(cols):
        for at_row in range(rows):
            head = ((row + at_row) % rows) * cols + (col + cols - at_col) % cols
            at = (at_col * rows + at_row) * HEAD_DIM
            left[at:at + HEAD_DIM, :] = back[head]
    turned = left[...].T
    hidden[:, pl.ds(pl.multiple_of(core * half, half), half)] = matmul(turned, mine[...].reshape(D, half), 1, 0)
    hidden[:, pl.ds(pl.multiple_of((1 - core) * half, half), half)] = matmul(
        turned, other[...].reshape(D, half), 1, 0)
    total = residual[...].reshape(count, D).astype(jnp.float32) + hidden[...]
    value = layer_norm(total, gain[...]).astype(jnp.bfloat16)
    group = out.shape[2]
    for index in range(out.shape[1]):
        for spot in range(4):
            at = (index * 4 + spot) * group
            out[spot, index] = value[at:at + group, :]


def merge_rows(place, back, row_tokens, mine, other, gain):
    cols, count, _ = row_tokens.shape
    return pl.pallas_call(
        hidden_kernel,
        out_shape=jax.ShapeDtypeStruct((4, cols, count // 4, D), jnp.bfloat16),
        grid_spec=pltpu.PrefetchScalarGridSpec(
            num_scalar_prefetch=1,
            grid=(cols // 2,),
            in_specs=[
                pl.BlockSpec((HEADS, HEAD_DIM, 2 * count), lambda i, p: (0, 0, i)),
                pl.BlockSpec((2, count, D), lambda i, p: (i, 0, 0)),
                whole(mine.shape), whole(other.shape), whole((D,)),
            ],
            out_specs=pl.BlockSpec((4, 2, count // 4, D), lambda i, p: (0, i, 0, 0)),
            scratch_shapes=[pltpu.VMEM((D, 2 * count), jnp.bfloat16), pltpu.VMEM((2 * count, D), jnp.float32)],
        ),
        name="merge_rows",
    )(place, back, row_tokens, mine, other, gain)


def merge_kernel(place, mine, other, own, *rest):
    parts, out, near, far = rest[:-3], rest[-3], rest[-2], rest[-1]
    core, parity = place[1], place[3]
    lanes = parts[0].shape[1]
    count, depth = mine.shape[1], 2 * D
    for index, source in enumerate((mine, other)):
        for spot in range(2):
            at = (slice(index * count, (index + 1) * count), slice(spot * D, (spot + 1) * D))
            near[at] = source[parity * 2 + spot]
            far[at] = source[2 - parity * 2 + spot]
    column = pl.ds(pl.multiple_of(core * lanes, lanes), lanes)
    near_own = own[pl.ds(pl.multiple_of(parity * depth, depth), depth), column]
    far_own = own[pl.ds(pl.multiple_of((1 - parity) * depth, depth), depth), column]
    near_wide = jnp.concatenate([near_own] + [part[...] for part in parts[0::2]], axis=1)
    far_wide = jnp.concatenate([far_own] + [part[...] for part in parts[1::2]], axis=1)
    value = matmul(near[...], near_wide, 1, 0) + matmul(far[...], far_wide, 1, 0)
    out[core] = value[0:count, :].astype(jnp.bfloat16)
    out[1 - core] = value[count:2 * count, :].astype(jnp.bfloat16)


def merge(place, mine, other, own, parts):
    width = parts[0].shape[1] * (1 + len(parts) // 2)
    return pl.pallas_call(
        merge_kernel,
        out_shape=jax.ShapeDtypeStruct((2, mine.shape[1], width), jnp.bfloat16),
        grid_spec=pltpu.PrefetchScalarGridSpec(
            num_scalar_prefetch=1,
            grid=(1,),
            in_specs=[whole(mine.shape), whole(other.shape), whole(own.shape)]
            + [whole(part.shape) for part in parts],
            out_specs=whole((2, mine.shape[1], width)),
            scratch_shapes=[pltpu.VMEM((2 * mine.shape[1], 2 * D), jnp.bfloat16)] * 2,
        ),
        name="merge",
    )(place, mine, other, own, *parts)


BACK_BY = (0, 1, 3, 2)


def place_kernel(place, got, out):
    cores, cols, _, wide = got.shape
    rows = len(BACK_BY)
    lanes = wide // rows
    for at_core in range(cores):
        for at_col in range(cols):
            for index, back_by in enumerate(BACK_BY):
                at = ((((place[0] + rows - back_by) % rows) * cols + at_col) * cores + at_core) * lanes
                out[:, pl.ds(pl.multiple_of(at, lanes), lanes)] = got[
                    at_core, at_col, :, index * lanes:(index + 1) * lanes]


def place_columns(place, got):
    cores, cols, count, wide = got.shape
    return pl.pallas_call(
        place_kernel,
        out_shape=jax.ShapeDtypeStruct((count, cores * cols * wide), jnp.bfloat16),
        grid_spec=pltpu.PrefetchScalarGridSpec(
            num_scalar_prefetch=1, grid=(1,), in_specs=[whole(got.shape)],
            out_specs=whole((count, cores * cols * wide))),
        name="place_columns",
    )(place, got)


def block_step(tokens, segment_ids, w_qkv, w_out, w_merge, gain_attn, gain_merge):
    rows, cols, planes = lax.axis_size("y"), lax.axis_size("x"), lax.axis_size("z")
    row, col, core = lax.axis_index("y"), lax.axis_index("x"), lax.axis_index("c")
    parity = lax.axis_index("z") % 2
    tok_local = tokens.shape[0]
    groups = tok_local // 4
    row_count = cols * tok_local
    half = D // 2
    wide = w_qkv.shape[1]
    place = jnp.stack([row, core, col, parity]).astype(jnp.int32)
    segments = segment_ids.reshape(rows * cols, groups, 4).transpose(0, 2, 1).reshape(-1)
    layout = attention_inputs(segments, segment_ids)
    row_tokens = lax.all_to_all(
        spread_tokens(tokens, cols), "x", split_axis=0, concat_axis=0, tiled=True)

    weights = w_qkv.T
    own = jnp.concatenate([
        lax.dynamic_slice_in_dim(weights, core * half, half, 1),
        lax.dynamic_slice_in_dim(w_out, core * half, half, 1)], axis=0)
    ahead = [shift_rows(own, step, rows) for step in (3, 2, 1)]
    other_qkv = swap_cores(jnp.stack([part[:wide] for part in ahead]))

    piece = (w_merge.shape[0] // 2, w_merge.shape[1] // 2)
    own_piece = lax.dynamic_slice(w_merge, (parity * piece[0], core * piece[1]), piece)
    first_y = shift_rows(own_piece, 1, rows)
    third_y = shift_rows(own_piece, 3, rows)

    qkv = project_qkv(
        place, row_tokens, gain_attn, weights, ahead, other_qkv, rows)
    by_head = lax.all_to_all(qkv, "y", split_axis=0, concat_axis=0, tiled=True)

    out_rows = jnp.stack([own[wide:]] + [part[wide:] for part in ahead])
    next_out = shift_cols(out_rows, 1, cols)
    out_parts = [out_rows, next_out] + [shift_cols(out_rows, step, cols) for step in (2, 3)]
    first_z = swap_planes(first_y, planes)
    third_z = swap_planes(third_y, planes)
    second_y = shift_rows(first_y, 1, rows)

    attended = attention(by_head, layout, cols)
    back = lax.all_to_all(
        attended.reshape(rows * cols, HEAD_DIM, row_count), ("y", "x"),
        split_axis=0, concat_axis=0, tiled=True)
    second_z = swap_planes(second_y, planes)
    mine_out = jnp.stack(out_parts)
    other_out = swap_cores(mine_out)
    merged = merge_rows(
        place, back, row_tokens, mine_out, other_out, gain_merge)
    merged = merged.reshape(4, cols * groups, D)
    other_merged = swap_cores(merged)
    block = merge(
        place, merged, other_merged, w_merge, (first_y, first_z, third_y, third_z, second_y, second_z))
    got = lax.all_to_all(
        block.reshape(2 * cols, groups, block.shape[2]), ("c", "x"), split_axis=0, concat_axis=0, tiled=True)
    return place_columns(place, got.reshape(2, cols, groups, block.shape[2]))


def solution(mesh):
    torus = Mesh(mesh.devices.reshape(mesh.shape["dp"] // 2, 2, 4, 4), ("z", "c", "y", "x"))
    dp, seq, both = ("z", "c"), ("y", "x"), ("z", "c", "y", "x")
    in_specs = (P(both, None), P(dp), P(None, seq), P(seq, None), P(None, seq), P(), P())
    return jax.shard_map(block_step, mesh=torus, in_specs=in_specs, out_specs=P(both, None), check_vma=False)
```
